32 devices in a mesh: ctx: 8 (over z, y), head: 4 (over x, core).
Axes of the slice: x: 2, y: 2, z: 4, core: 2. Of those that a mesh axis runs over, the one named last changes fastest.
Arguments:
- queries: bfloat16 [512, 8192], P('ctx', 'head'), may hold values from -6 to 6
- draft_node_keys: bfloat16 [512, 1024], P('ctx', 'head'), may hold values from -4 to 4
- draft_node_values: bfloat16 [512, 1024], P('ctx', 'head'), may hold values from -6 to 6
- prompt_keys: bfloat16 [2, 8192, 1024], P(None, 'ctx', 'head'), may hold values from -6 to 6
- prompt_values: bfloat16 [2, 8192, 1024], P(None, 'ctx', 'head'), may hold values from -6 to 6
- request_group: int32 [8], replicated, may hold values from 0 to 1
- parents: int32 [8, 64], P('ctx'), may hold values from 0 to 62, as said below
- node_visibility_mask: int32 [8, 64, 64], P('ctx'), may hold values from 0 to 1, as said below
- path_nodes: int32 [8, 8], P('ctx'), may hold values from 0 to 21, as said below
- path_lengths: int32 [8], replicated, may hold values from 1 to 8, 32 in all
- fc_node: bfloat16 [8192, 8192], P('head', 'ctx'), may hold values from -0.046875 to 0.046875
- fc_parent: bfloat16 [8192, 8192], P('head', 'ctx'), may hold values from -0.046875 to 0.046875
- norm_gain: float32 [8192], P('ctx'), may hold values from 0.5 to 1.5
- w_gate: bfloat16 [8192, 28672], P('ctx', 'head'), may hold values from -0.0625 to 0.0625
- w_up: bfloat16 [8192, 28672], P('ctx', 'head'), may hold values from -0.0625 to 0.0625
- w_down: bfloat16 [28672, 8192], P('head', 'ctx'), may hold values from -0.03125 to 0.03125
Outputs:
- attn_out: bfloat16 [512, 8192], P('ctx', 'head')
- draft_out: bfloat16 [64, 8192], P('head', 'ctx')
The draws below stay inside these ranges and needn't reach their ends.
Inputs may be any that keep to these rules, and one draw needn't show every extreme that they name: parents[r, 0] is 0, the root; for n > 0, parents[r, n] lies in n - 3 to n - 1. node_visibility_mask[r, n, j] is 1 exactly when j is n or an ancestor of n under parents[r]. path_nodes[r, 0] is 0, and for 0 < k < 8 the parent of path_nodes[r, k] is path_nodes[r, k - 1], so path_nodes[r, k] lies in k to 3 * k. `path_lengths`: the lengths sum to 32 and the largest is 8.
All inputs are finite; a program needn't handle non-finite values.
Results may differ from the reference program's by a relative error of at most 0.0096.
Values may be sent and summed in bfloat16 or wider, within the bound.
No kernel may reach another device: no remote copies, remote signals or barrier semaphores. Data moves between devices by JAX's collectives and lax.ppermute only.
A program may use at most 192 MiB of HBM per device.

```python
import math
import jax
import jax.numpy as jnp
import numpy as np
from jax import lax

MODEL_WIDTH = 8192
QUERY_HEAD_COUNT = 64
KEY_VALUE_HEADS = 8
HEAD_SIZE = 128
FF = 28672
TREE_NODES = 64
ACCEPT = 8
CONTEXT_PROMPT = 1024
PROMPT_GROUPS = 2
PROMPT_POSITIONS = 8192
REQUEST_TOTAL = 8
PATH_ROWS = 64
LIVE_ROWS = 32
N_CTX = 8


def tree_draw(key):
    tree_key = jax.random.fold_in(key, 97)
    node_index = jnp.arange(TREE_NODES, dtype=jnp.int32)
    request_index = jnp.arange(REQUEST_TOTAL, dtype=jnp.int32)
    gap_draw = jax.random.randint(jax.random.fold_in(tree_key, 1), (REQUEST_TOTAL, TREE_NODES), 1, 4)
    gap_draw = jnp.where(request_index[:, None] == 0, 3, gap_draw)
    parents = node_index[None, :] - jnp.minimum(gap_draw, node_index[None, :])

    def deepen(turn_idx, node_depth):
        return jnp.where(node_index[None, :] > 0, jnp.take_along_axis(node_depth, parents, axis=1) + 1, 0)
    node_depth = lax.fori_loop(0, TREE_NODES, deepen, jnp.zeros((REQUEST_TOTAL, TREE_NODES), jnp.int32))

    def climb(turn_idx, carry):
        ancestry, climber = carry
        ancestry = jnp.maximum(ancestry, (climber[:, :, None] == node_index[None, None, :]).astype(jnp.int32))
        return (ancestry, jnp.take_along_axis(parents, climber, axis=1))
    start_anc = jnp.zeros((REQUEST_TOTAL, TREE_NODES, TREE_NODES), jnp.int32)
    start_climb = jnp.broadcast_to(node_index[None, :], (REQUEST_TOTAL, TREE_NODES))
    ancestry, unused = lax.fori_loop(0, TREE_NODES, climb, (start_anc, start_climb))
    target = TREE_NODES - 1 - jax.random.randint(jax.random.fold_in(tree_key, 2), (REQUEST_TOTAL,), 0, max(TREE_NODES // 8, 1))
    target = jnp.where(request_index == 0, (TREE_NODES - 1) // 3 * 3, target)
    target_hot = (node_index[None, :] == target[:, None]).astype(jnp.int32)
    lineage = jnp.sum(ancestry * target_hot[:, :, None], axis=1)
    levels = jnp.arange(ACCEPT, dtype=jnp.int32)
    on_level = (node_depth[:, None, :] == levels[None, :, None]).astype(jnp.int32)
    path_nodes = jnp.sum(node_index[None, None, :] * lineage[:, None, :] * on_level, axis=2)
    return (parents.astype(jnp.int32), ancestry.astype(jnp.int32), path_nodes.astype(jnp.int32))


def draw_parents(key, part):
    return tree_draw(key)[0]


def draw_node_visibility_mask(key, part):
    return tree_draw(key)[1]


def draw_path_nodes(key, part):
    return tree_draw(key)[2]


def draw_queries(key, part):
    dimension_shape = (REQUEST_TOTAL, TREE_NODES, QUERY_HEAD_COUNT, HEAD_SIZE)
    base_sample = jnp.clip(jax.random.normal(jax.random.fold_in(key, 5), dimension_shape, jnp.float32), -6.0, 6.0)
    return base_sample.reshape(REQUEST_TOTAL * TREE_NODES, QUERY_HEAD_COUNT * HEAD_SIZE).astype(jnp.bfloat16)


def draw_draft_node_keys(key, part):
    dimension_shape = (REQUEST_TOTAL, TREE_NODES, KEY_VALUE_HEADS, HEAD_SIZE)
    base_sample = jnp.clip(jax.random.normal(jax.random.fold_in(key, 9), dimension_shape, jnp.float32), -4.0, 4.0)
    return base_sample.reshape(REQUEST_TOTAL * TREE_NODES, KEY_VALUE_HEADS * HEAD_SIZE).astype(jnp.bfloat16)


def draw_prompt_keys(key, part):
    dimension_shape = (PROMPT_GROUPS, PROMPT_POSITIONS, KEY_VALUE_HEADS, HEAD_SIZE)
    base_sample = jnp.clip(jax.random.normal(jax.random.fold_in(key, 31), dimension_shape, jnp.float32), -6.0, 6.0)
    return base_sample.reshape(PROMPT_GROUPS, PROMPT_POSITIONS, KEY_VALUE_HEADS * HEAD_SIZE).astype(jnp.bfloat16)


def set_ends(drawn, own_key, least, top_value):
    spot = [jax.random.randint(jax.random.fold_in(own_key, axis), (), 0, length) for axis, length in enumerate(drawn.shape)]
    widest = drawn.shape.index(max(drawn.shape))
    neighbour = spot[:widest] + [(spot[widest] + 1) % drawn.shape[widest]] + spot[widest + 1:]
    return drawn.at[tuple(spot)].set(least).at[tuple(neighbour)].set(top_value)


def block_scale(stream_key, extent, pieces, smallest, largest):
    def one(position, blocks):
        steps = jax.random.uniform(jax.random.fold_in(jax.random.fold_in(stream_key, 6), position), (blocks,), jnp.float32, smallest / len(pieces), largest / len(pieces))
        return jnp.repeat(jnp.exp(steps), extent[position] // blocks).reshape((-1,) + (1,) * (len(extent) - position - 1))

    factor_of = one(*pieces[0])
    for cut in pieces[1:]:
        factor_of = factor_of * one(*cut)
    return factor_of


def split_up(number_of, total, limit, lean):
    portions = [(1 << 20) // math.isqrt(grade ** lean) + 1 for grade in range(2, number_of + 1)]
    rest, holding = total - limit - (number_of - 1), [1] * (number_of - 1)
    while rest > 0:
        movable = [i for i in range(number_of - 1) if holding[i] < limit]
        pool, remaining = sum([portions[i] for i in movable]), rest
        for i in movable:
            more = min(limit - holding[i], max(1, remaining * portions[i] // pool), rest)
            holding[i] = holding[i] + more
            rest = rest - more
    return np.array([limit] + holding)


def ragged(key, number_of, total, most, skew):
    if number_of == 2:
        one = jax.random.randint(key, (), max(1, total - most), min(most, total - 1) + 1)
        return jnp.stack([one, total - one])
    tallies = jnp.asarray(split_up(number_of, total, most, skew), jnp.int32)
    twos = (number_of - 1) // 2
    giver, sink = tallies[1:1 + 2 * twos:2], tallies[2:2 + 2 * twos:2]
    margin = jnp.minimum(giver - 1, most - sink)
    passed = jax.random.randint(jax.random.fold_in(key, 1), (twos,), 0, 1 << 20) % (margin + 1)
    tallies = tallies.at[1:1 + 2 * twos:2].set(giver - passed).at[2:2 + 2 * twos:2].set(sink + passed)
    return tallies[jax.random.permutation(jax.random.fold_in(key, 2), number_of)]


def normal_values(own_key, shape, deviation, limit, cuts=(), kind=jnp.bfloat16):
    drawn = deviation * jax.random.normal(own_key, shape, jnp.float32)
    if cuts:
        drawn = drawn * block_scale(own_key, shape, cuts, -0.22, 0.18)
    return jnp.clip(drawn, -limit, limit).astype(kind)


def setup_inputs(seed: int = 0) -> dict:
    seeds = jax.random.split(jax.random.key(seed), 17)
    queries = draw_queries(jax.random.fold_in(seeds[16], 71), 0)
    draft_node_keys = draw_draft_node_keys(jax.random.fold_in(seeds[16], 71), 0)
    draft_node_values = normal_values(seeds[2], (REQUEST_TOTAL * TREE_NODES, KEY_VALUE_HEADS * HEAD_SIZE), 1.0, 6.0, ((0, 8), (1, 4)))
    prompt_keys = draw_prompt_keys(jax.random.fold_in(seeds[16], 71), 0)
    prompt_values = normal_values(seeds[4], (PROMPT_GROUPS, PROMPT_POSITIONS, KEY_VALUE_HEADS * HEAD_SIZE), 1.0, 6.0, ((1, 8), (2, 4)))
    request_group = set_ends(jax.random.randint(seeds[5], (REQUEST_TOTAL,), 0, PROMPT_GROUPS), jax.random.fold_in(seeds[5], 1), 0, PROMPT_GROUPS - 1).astype(jnp.int32)
    parents = draw_parents(jax.random.fold_in(seeds[16], 71), 0)
    node_visibility_mask = draw_node_visibility_mask(jax.random.fold_in(seeds[16], 71), 0)
    path_nodes = draw_path_nodes(jax.random.fold_in(seeds[16], 71), 0)
    path_lengths = ragged(seeds[9], REQUEST_TOTAL, LIVE_ROWS, ACCEPT, 1).astype(jnp.int32)
    fc_node = normal_values(seeds[10], (MODEL_WIDTH, MODEL_WIDTH), (2 * MODEL_WIDTH) ** -0.5, 0.046875, ((0, 4), (1, 8)))
    fc_parent = normal_values(seeds[11], (MODEL_WIDTH, MODEL_WIDTH), (2 * MODEL_WIDTH) ** -0.5, 0.046875, ((0, 4), (1, 8)))
    norm_gain = jnp.clip(1.0 + 0.1 * jax.random.normal(seeds[12], (MODEL_WIDTH,), jnp.float32), 0.5, 1.5)
    w_gate = normal_values(seeds[13], (MODEL_WIDTH, FF), MODEL_WIDTH ** -0.5, 0.0625, ((0, 8), (1, 4)))
    w_up = normal_values(seeds[14], (MODEL_WIDTH, FF), MODEL_WIDTH ** -0.5, 0.0625, ((0, 8), (1, 4)))
    w_down = normal_values(seeds[15], (FF, MODEL_WIDTH), FF ** -0.5, 0.03125, ((0, 4), (1, 8)))
    return {"queries": queries, "draft_node_keys": draft_node_keys, "draft_node_values": draft_node_values, "prompt_keys": prompt_keys, "prompt_values": prompt_values, "request_group": request_group, "parents": parents, "node_visibility_mask": node_visibility_mask, "path_nodes": path_nodes, "path_lengths": path_lengths, "fc_node": fc_node, "fc_parent": fc_parent, "norm_gain": norm_gain, "w_gate": w_gate, "w_up": w_up, "w_down": w_down}


def pick_rows(feature_rows, row_ids):
    return jnp.take(feature_rows, row_ids, axis=0)

def reference(queries, draft_node_keys, draft_node_values, prompt_keys, prompt_values, request_group, parents, node_visibility_mask, path_nodes, path_lengths, fc_node, fc_parent, norm_gain, w_gate, w_up, w_down):
    repeat_heads = QUERY_HEAD_COUNT // KEY_VALUE_HEADS
    score_scale = HEAD_SIZE ** (-0.5)

    def single_request(block_args):
        query_matrix, prompt_group, gathered_key_rows, gathered_value_rows, mask_rows = block_args
        full_query = query_matrix.astype(jnp.float32).reshape(TREE_NODES, KEY_VALUE_HEADS, repeat_heads, HEAD_SIZE)
        selected_keys = lax.dynamic_index_in_dim(prompt_keys, prompt_group, 0, keepdims=False).reshape(N_CTX, CONTEXT_PROMPT, KEY_VALUE_HEADS, HEAD_SIZE)
        selected_values = lax.dynamic_index_in_dim(prompt_values, prompt_group, 0, keepdims=False).reshape(N_CTX, CONTEXT_PROMPT, KEY_VALUE_HEADS, HEAD_SIZE)

        def one_shard(shard_args):
            shard_keys, shard_values = shard_args
            scores = jnp.einsum('nkad,pkd->kanp', full_query, shard_keys.astype(jnp.float32)) * score_scale
            shard_top = lax.optimization_barrier(jnp.max(scores, axis=-1))
            weights = jnp.exp(scores - shard_top[..., None])
            shard_sum = lax.optimization_barrier(jnp.sum(weights, axis=-1))
            rounded = lax.optimization_barrier(weights.astype(jnp.bfloat16)).astype(jnp.float32)
            mixture = jnp.einsum('kanp,pkd->nkad', rounded, shard_values.astype(jnp.float32))
            shard_out = (mixture / jnp.transpose(shard_sum, (2, 0, 1))[..., None]).astype(jnp.bfloat16)
            return (shard_out, shard_top, shard_sum)
        source_out, source_top, source_sum = lax.map(one_shard, (selected_keys, selected_values))
        node_key_rows = gathered_key_rows.astype(jnp.float32).reshape(TREE_NODES, KEY_VALUE_HEADS, HEAD_SIZE)
        node_value_rows = gathered_value_rows.astype(jnp.float32).reshape(TREE_NODES, KEY_VALUE_HEADS, HEAD_SIZE)
        allowed = (mask_rows > 0)[None, None]
        tree_scores = jnp.einsum('nkad,jkd->kanj', full_query, node_key_rows) * score_scale
        tree_scores = jnp.where(allowed, tree_scores, -1e+30)
        tree_top = lax.optimization_barrier(jnp.max(tree_scores, axis=-1))
        tree_weights = jnp.where(allowed, jnp.exp(tree_scores - tree_top[..., None]), 0.0)
        tree_sum = lax.optimization_barrier(jnp.sum(tree_weights, axis=-1))
        tree_rounded = lax.optimization_barrier(tree_weights.astype(jnp.bfloat16)).astype(jnp.float32)
        tree_out = jnp.einsum('kanj,jkd->nkad', tree_rounded, node_value_rows)
        best_top = jnp.maximum(lax.optimization_barrier(jnp.max(source_top, axis=0)), tree_top)
        source_weight = jnp.transpose(source_sum * jnp.exp(source_top - best_top[None]), (0, 3, 1, 2))
        tree_scale = jnp.exp(tree_top - best_top)
        tree_weight = jnp.transpose(tree_scale, (2, 0, 1))
        tree_total = jnp.transpose(tree_scale * tree_sum, (2, 0, 1))
        numerator = lax.optimization_barrier(jnp.sum(source_weight[..., None] * source_out.astype(jnp.float32), axis=0)) + tree_weight[..., None] * tree_out
        denominator = lax.optimization_barrier(jnp.sum(source_weight, axis=0)) + tree_total
        return (numerator / denominator[..., None]).astype(jnp.bfloat16).reshape(TREE_NODES, MODEL_WIDTH)
    attention_fn = lax.map(single_request, (queries.reshape(REQUEST_TOTAL, TREE_NODES, MODEL_WIDTH), request_group, draft_node_keys.reshape(REQUEST_TOTAL, TREE_NODES, KEY_VALUE_HEADS * HEAD_SIZE), draft_node_values.reshape(REQUEST_TOTAL, TREE_NODES, KEY_VALUE_HEADS * HEAD_SIZE), node_visibility_mask))
    attn_out = attention_fn.reshape(REQUEST_TOTAL * TREE_NODES, MODEL_WIDTH)
    parent_nodes = jnp.take_along_axis(parents, path_nodes, axis=1)
    node_rows = jax.vmap(pick_rows)(attention_fn, path_nodes)
    parent_rows = jax.vmap(pick_rows)(attention_fn, parent_nodes)
    is_live = (jnp.arange(ACCEPT)[None, :] < path_lengths[:, None])[..., None]
    node_rows = jnp.where(is_live, node_rows, jnp.zeros_like(node_rows)).reshape(PATH_ROWS, MODEL_WIDTH)
    parent_rows = jnp.where(is_live, parent_rows, jnp.zeros_like(parent_rows)).reshape(PATH_ROWS, MODEL_WIDTH)
    draft_x = jnp.dot(node_rows, fc_node, preferred_element_type=jnp.float32) + jnp.dot(parent_rows, fc_parent, preferred_element_type=jnp.float32)
    mean_square = lax.optimization_barrier(jnp.mean(draft_x * draft_x, axis=-1))
    draft_norm = (draft_x * lax.rsqrt(mean_square + 1e-05)[:, None] * norm_gain[None, :]).astype(jnp.bfloat16)
    gate = jnp.dot(draft_norm, w_gate, preferred_element_type=jnp.float32)
    up_part = jnp.dot(draft_norm, w_up, preferred_element_type=jnp.float32)
    hidden = (jax.nn.silu(gate) * up_part).astype(jnp.bfloat16)
    draft_out = (draft_x + jnp.dot(hidden, w_down, preferred_element_type=jnp.float32)).astype(jnp.bfloat16)
    return (attn_out, draft_out)
```

```python
import functools

import jax
import jax.numpy as jnp
from jax import lax
from jax.experimental import pallas as pl
from jax.experimental.pallas import tpu as pltpu
from jax.sharding import PartitionSpec as P

MODEL_WIDTH = 8192
HEAD_SIZE = 128
TREE_NODES = 64
ACCEPT = 8
LANES = 128
LOG2E = 1.4426950408889634
SCORE_BASE2 = HEAD_SIZE ** (-0.5) * LOG2E

BF16 = jnp.bfloat16
F32 = jnp.float32


def dot_nt(a, b):
    return lax.dot_general(a, b, (((1,), (1,)), ((), ())), preferred_element_type=F32)


def dot_nn(a, b):
    return lax.dot_general(a, b, (((1,), (0,)), ((), ())), preferred_element_type=F32)


def split_lanes(stat, width):
    hi = stat.astype(BF16).astype(F32)
    mid = (stat - hi).astype(BF16).astype(F32)
    lo = (stat - hi - mid).astype(BF16).astype(F32)
    packed = hi + pltpu.roll(mid, width, 1) + pltpu.roll(lo, 2 * width, 1)
    return packed.astype(BF16)


def join_lanes(packed, width):
    wide = packed.astype(F32)
    return (
        wide + pltpu.roll(wide, LANES - width, 1) + pltpu.roll(wide, LANES - 2 * width, 1)
    )


def vmem(limit_mib):
    return pltpu.CompilerParams(vmem_limit_bytes=limit_mib << 20)


def shard_rows(q_heads, score_fn, mix_fn):
    q = jnp.concatenate(q_heads, axis=0)
    raw = score_fn(q)
    top = jnp.max(raw, axis=1, keepdims=True) * SCORE_BASE2
    weights = jnp.exp2(raw * SCORE_BASE2 - top)
    total = jnp.sum(weights, axis=1, keepdims=True)
    out = (mix_fn(weights) / total).astype(BF16)
    return out, top + jnp.log(total) * LOG2E


def bulk_kernel(group_ref, q_ref, k_ref, v_ref, o_ref, *, kv_heads, repeat, step):
    nodes = q_ref.shape[1]
    heads = kv_heads * repeat
    group = group_ref[pl.program_id(0)]
    lane = lax.broadcasted_iota(jnp.int32, (nodes, LANES), 1)
    stat = jnp.zeros((nodes, LANES), F32)
    for k in range(kv_heads):
        cols = slice(k * HEAD_SIZE, (k + 1) * HEAD_SIZE)
        keys = k_ref[group, :, cols]
        values = v_ref[group, :, cols]
        for first in range(k * repeat, (k + 1) * repeat, step):
            out, lse = shard_rows(
                [
                    q_ref[0, :, h * HEAD_SIZE : (h + 1) * HEAD_SIZE]
                    for h in range(first, first + step)
                ],
                lambda q: dot_nt(q, keys),
                lambda w: dot_nn(w.astype(BF16), values),
            )
            for i in range(step):
                h = first + i
                rows = slice(i * nodes, (i + 1) * nodes)
                o_ref[0, :, h * HEAD_SIZE : (h + 1) * HEAD_SIZE] = out[rows]
                stat = jnp.where(lane == h, lse[rows], stat)
    o_ref[0, :, heads * HEAD_SIZE :] = split_lanes(stat, heads)


def bulk_attend(queries, keys, values, groups, kv_heads, repeat):
    requests, nodes, width = queries.shape
    out_width = width + LANES
    span = keys.shape[1]
    work = requests * nodes * span * width
    return pl.pallas_call(
        functools.partial(bulk_kernel, kv_heads=kv_heads, repeat=repeat, step=min(4, repeat)),
        out_shape=jax.ShapeDtypeStruct((requests, nodes, out_width), BF16),
        grid_spec=pltpu.PrefetchScalarGridSpec(
            num_scalar_prefetch=1,
            grid=(requests,),
            in_specs=[
                pl.BlockSpec((1, nodes, width), lambda r, g: (r, 0, 0)),
                pl.BlockSpec(keys.shape, lambda r, g: (0, 0, 0)),
                pl.BlockSpec(values.shape, lambda r, g: (0, 0, 0)),
            ],
            out_specs=pl.BlockSpec((1, nodes, out_width), lambda r, g: (r, 0, 0)),
        ),
        compiler_params=vmem(40),
        cost_estimate=pl.CostEstimate(
            flops=4 * work, bytes_accessed=8 << 20, transcendentals=work // HEAD_SIZE
        ),
        name="bulk_attend",
    )(groups, queries, keys, values)


def path_kernel(group_ref, q_ref, k_ref, v_ref, o_ref, *, kv_heads, repeat, step, per_block):
    rows_block = q_ref.shape[0]
    heads = kv_heads * repeat
    lane = lax.broadcasted_iota(jnp.int32, (rows_block, LANES), 1)
    owner = lax.broadcasted_iota(jnp.int32, (rows_block, 1), 0) // ACCEPT
    row_group = jnp.zeros((rows_block, 1), jnp.int32)
    for i in range(per_block):
        row_group = jnp.where(
            owner == i, group_ref[pl.program_id(0) * per_block + i], row_group
        )
    first_group = jnp.concatenate([row_group] * step, axis=0) == 0
    stat = jnp.zeros((rows_block, LANES), F32)
    for k in range(kv_heads):
        cols = slice(k * HEAD_SIZE, (k + 1) * HEAD_SIZE)
        for first in range(k * repeat, (k + 1) * repeat, step):
            out, lse = shard_rows(
                [
                    q_ref[:, h * HEAD_SIZE : (h + 1) * HEAD_SIZE]
                    for h in range(first, first + step)
                ],
                lambda q: jnp.where(
                    first_group, dot_nt(q, k_ref[0, :, cols]), dot_nt(q, k_ref[1, :, cols])
                ),
                lambda w: jnp.where(
                    first_group,
                    dot_nn(w.astype(BF16), v_ref[0, :, cols]),
                    dot_nn(w.astype(BF16), v_ref[1, :, cols]),
                ),
            )
            for i in range(step):
                h = first + i
                rows = slice(i * rows_block, (i + 1) * rows_block)
                o_ref[:, h * HEAD_SIZE : (h + 1) * HEAD_SIZE] = out[rows]
                stat = jnp.where(lane == h, lse[rows], stat)
    o_ref[:, heads * HEAD_SIZE :] = split_lanes(stat, heads)


def path_attend(rows_all, keys, values, groups, kv_heads, repeat):
    rows, width = rows_all.shape
    out_width = width + LANES
    per_block = 8
    block = per_block * ACCEPT
    work = rows * keys.shape[1] * width
    return pl.pallas_call(
        functools.partial(
            path_kernel,
            kv_heads=kv_heads,
            repeat=repeat,
            step=min(4, repeat),
            per_block=per_block,
        ),
        out_shape=jax.ShapeDtypeStruct((rows, out_width), BF16),
        grid_spec=pltpu.PrefetchScalarGridSpec(
            num_scalar_prefetch=1,
            grid=(rows // block,),
            in_specs=[
                pl.BlockSpec((block, width), lambda r, g: (r, 0)),
                pl.BlockSpec(keys.shape, lambda r, g: (0, 0, 0)),
                pl.BlockSpec(values.shape, lambda r, g: (0, 0, 0)),
            ],
            out_specs=pl.BlockSpec((block, out_width), lambda r, g: (r, 0)),
        ),
        compiler_params=vmem(40),
        cost_estimate=pl.CostEstimate(
            flops=8 * work, bytes_accessed=3 << 20, transcendentals=work // HEAD_SIZE
        ),
        name="path_attend",
    )(groups, rows_all, keys, values)


def combine_kernel(recv_ref, stat_ref, q_ref, k_ref, v_ref, mask_ref, o_ref, *, repeat, heads):
    sources, rows, _ = recv_ref.shape
    copies = o_ref.shape[0]
    k = pl.program_id(0)
    stats = [join_lanes(stat_ref[c], heads) for c in range(sources)]
    best_src = functools.reduce(jnp.maximum, stats)
    q = jnp.concatenate(
        [q_ref[:, i * HEAD_SIZE : (i + 1) * HEAD_SIZE].astype(F32) for i in range(repeat)],
        axis=0,
    ).astype(BF16)
    allowed = jnp.concatenate([mask_ref[...]] * repeat, axis=0) > 0
    raw = jnp.where(allowed, dot_nt(q, k_ref[...]) * SCORE_BASE2, -1e30)
    top = jnp.max(raw, axis=1, keepdims=True)
    weights = jnp.where(allowed, jnp.exp2(raw - top), 0.0)
    total = jnp.sum(weights, axis=1, keepdims=True)
    mixed = dot_nn(weights.astype(BF16), v_ref[...])
    lane = lax.broadcasted_iota(jnp.int32, (rows, LANES), 1)
    for i in range(repeat):
        picked = lane == k * repeat + i
        own = slice(i * rows, (i + 1) * rows)

        def column(stat):
            return jnp.sum(jnp.where(picked, stat, 0.0), axis=1, keepdims=True)

        best = jnp.maximum(column(best_src), top[own])
        tree_scale = jnp.exp2(top[own] - best)
        numer = tree_scale * mixed[own]
        denom = tree_scale * total[own]
        for c in range(sources):
            scale = jnp.exp2(column(stats[c]) - best)
            numer += scale * recv_ref[c, :, i * HEAD_SIZE : (i + 1) * HEAD_SIZE].astype(F32)
            denom += scale
        out = (numer / denom).astype(BF16)
        for j in range(copies):
            o_ref[j, :, i * HEAD_SIZE : (i + 1) * HEAD_SIZE] = out


def combine(recv, queries, tree_keys, tree_values, mask, kv_heads, repeat, copies, name):
    sources, rows, wide = recv.shape
    width = wide - LANES
    part = repeat * HEAD_SIZE
    return pl.pallas_call(
        functools.partial(combine_kernel, repeat=repeat, heads=kv_heads * repeat),
        out_shape=jax.ShapeDtypeStruct((copies, rows, width), BF16),
        grid=(kv_heads,),
        in_specs=[
            pl.BlockSpec((sources, rows, part), lambda k: (0, 0, k)),
            pl.BlockSpec((sources, rows, LANES), lambda k: (0, 0, width // LANES)),
            pl.BlockSpec((rows, part), lambda k: (0, k)),
            pl.BlockSpec((TREE_NODES, HEAD_SIZE), lambda k: (0, k)),
            pl.BlockSpec((TREE_NODES, HEAD_SIZE), lambda k: (0, k)),
            pl.BlockSpec((rows, TREE_NODES), lambda k: (0, 0)),
        ],
        out_specs=pl.BlockSpec((copies, rows, part), lambda k: (0, 0, k)),
        compiler_params=vmem(40),
        cost_estimate=pl.CostEstimate(
            flops=4 * rows * width * TREE_NODES,
            bytes_accessed=2 * recv.size + 4 * rows * width,
            transcendentals=rows * width // 2,
        ),
        name=name,
    )(recv, recv, queries, tree_keys, tree_values, mask)


def fc_kernel(feat_ref, pick_ref, prev_ref, wn_ref, wp_ref, o_ref):
    feats = feat_ref[...]
    node = dot_nn(pick_ref[...], feats).astype(BF16)
    parent = dot_nn(prev_ref[...], feats).astype(BF16)
    part = dot_nn(node, wn_ref[...]) + dot_nn(parent, wp_ref[...])

    @pl.when(pl.program_id(0) == 0)
    def _():
        o_ref[...] = part

    @pl.when(pl.program_id(0) > 0)
    def _():
        o_ref[...] += part


def fc_project(feats, pick, prev, fc_node, fc_parent):
    slots, width = feats.shape
    live = pick.shape[0]
    cols = fc_node.shape[1]
    block = min(width, 512)
    return pl.pallas_call(
        fc_kernel,
        out_shape=jax.ShapeDtypeStruct((live, cols), F32),
        grid=(width // block,),
        in_specs=[
            pl.BlockSpec((slots, block), lambda i: (0, i)),
            pl.BlockSpec((live, slots), lambda i: (0, 0)),
            pl.BlockSpec((live, slots), lambda i: (0, 0)),
            pl.BlockSpec((block, cols), lambda i: (i, 0)),
            pl.BlockSpec((block, cols), lambda i: (i, 0)),
        ],
        out_specs=pl.BlockSpec((live, cols), lambda i: (0, 0)),
        compiler_params=vmem(40),
        cost_estimate=pl.CostEstimate(
            flops=4 * live * width * cols, bytes_accessed=4 * width * cols, transcendentals=0
        ),
        name="fc_project",
    )(feats, pick, prev, fc_node, fc_parent)


def gate_kernel(xa_ref, xb_ref, gain_ref, wg_ref, wu_ref, o_ref):
    x = xa_ref[...] + xb_ref[...]
    units = wg_ref.shape[1]
    scaled = (x * gain_ref[...]).astype(BF16)
    o_ref[0, :, :units] = dot_nn(scaled, wg_ref[...]).astype(BF16)
    o_ref[0, :, units : 2 * units] = dot_nn(scaled, wu_ref[...]).astype(BF16)
    squares = jnp.sum(x * x, axis=1, keepdims=True)
    lane = lax.broadcasted_iota(jnp.int32, (x.shape[0], LANES), 1)
    o_ref[0, :, 2 * units :] = split_lanes(jnp.where(lane == 0, squares, 0.0), 1)


def gate_up(xa, xb, gain, w_gate, w_up, parts):
    live, width = xa.shape
    units = w_gate.shape[1] // parts
    return pl.pallas_call(
        gate_kernel,
        out_shape=jax.ShapeDtypeStruct((parts, live, 2 * units + LANES), BF16),
        grid=(parts,),
        in_specs=[
            pl.BlockSpec((live, width), lambda i: (0, 0)),
            pl.BlockSpec((live, width), lambda i: (0, 0)),
            pl.BlockSpec((1, width), lambda i: (0, 0)),
            pl.BlockSpec((width, units), lambda i: (0, i)),
            pl.BlockSpec((width, units), lambda i: (0, i)),
        ],
        out_specs=pl.BlockSpec((1, live, 2 * units + LANES), lambda i: (i, 0, 0)),
        compiler_params=vmem(40),
        cost_estimate=pl.CostEstimate(
            flops=4 * live * width * units * parts,
            bytes_accessed=4 * width * units * parts,
            transcendentals=0,
        ),
        name="gate_up",
    )(xa, xb, gain, w_gate, w_up)


def act_kernel(recv_ref, o_ref):
    units = o_ref.shape[2]
    sources = recv_ref.shape[0]
    total = recv_ref[0].astype(F32)
    for c in range(1, sources):
        total += recv_ref[c].astype(F32)
    squares = jnp.sum(total[:, 2 * units :], axis=1, keepdims=True)
    scale = lax.rsqrt(squares / MODEL_WIDTH + 1e-05)
    gate = total[:, :units] * scale
    up = total[:, units : 2 * units] * scale
    hidden = (gate / (1.0 + jnp.exp(-gate)) * up).astype(BF16)
    for c in range(sources):
        o_ref[c] = hidden


def activate(recv):
    sources, live, wide = recv.shape
    units = (wide - LANES) // 2
    return pl.pallas_call(
        act_kernel,
        out_shape=jax.ShapeDtypeStruct((sources, live, units), BF16),
        compiler_params=vmem(40),
        cost_estimate=pl.CostEstimate(
            flops=recv.size, bytes_accessed=3 * recv.size, transcendentals=live * units
        ),
        name="activate",
    )(recv)


def down_kernel(head_ref, hid_ref, w_ref, xa_ref, xb_ref, spread_ref, o_ref, acc_ref):
    @pl.when(pl.program_id(0) == 0)
    def _():
        residual = xa_ref[...] + xb_ref[...]
        acc_ref[...] = jnp.where(head_ref[0] == 0, residual, 0.0)

    acc_ref[...] += dot_nn(hid_ref[0], w_ref[...])

    @pl.when(pl.program_id(0) == pl.num_programs(0) - 1)
    def _():
        o_ref[...] = lax.dot_general(
            spread_ref[...],
            acc_ref[...],
            (((1,), (0,)), ((), ())),
            precision=lax.Precision.HIGHEST,
            preferred_element_type=F32,
        )


def down_project(head, hidden, w_down, xa, xb, spread):
    parts, live, units = hidden.shape
    cols = w_down.shape[1]
    slots = spread.shape[0]
    return pl.pallas_call(
        down_kernel,
        out_shape=jax.ShapeDtypeStruct((slots, cols), F32),
        grid_spec=pltpu.PrefetchScalarGridSpec(
            num_scalar_prefetch=1,
            grid=(parts,),
            in_specs=[
                pl.BlockSpec((1, live, units), lambda i, h: (i, 0, 0)),
                pl.BlockSpec((units, cols), lambda i, h: (i, 0)),
                pl.BlockSpec((live, cols), lambda i, h: (0, 0)),
                pl.BlockSpec((live, cols), lambda i, h: (0, 0)),
                pl.BlockSpec((slots, live), lambda i, h: (0, 0)),
            ],
            out_specs=pl.BlockSpec((slots, cols), lambda i, h: (0, 0)),
            scratch_shapes=[pltpu.VMEM((live, cols), F32)],
        ),
        compiler_params=vmem(40),
        cost_estimate=pl.CostEstimate(
            flops=2 * live * parts * units * cols,
            bytes_accessed=2 * parts * units * cols,
            transcendentals=0,
        ),
        name="down_project",
    )(head, hidden, w_down, xa, xb, spread)


def swap(blocks, axis):
    return lax.all_to_all(blocks, axis, split_axis=0, concat_axis=0, tiled=True)


def spread_all(block, axis):
    count = lax.axis_size(axis)
    return swap(jnp.broadcast_to(block[None], (count,) + block.shape), axis)


def partner(value, axis, distance):
    count = lax.axis_size(axis)
    return lax.ppermute(value, axis, [(i, i ^ distance) for i in range(count)])


def live_rows(path_lengths):
    requests = path_lengths.shape[0]
    slots = requests * ACCEPT
    live = slots // 2
    index = jnp.arange(requests)
    starts = jnp.sum(
        jnp.where(index[None, :] < index[:, None], path_lengths[None, :], 0), axis=1
    )
    step = jnp.arange(ACCEPT)
    place = jnp.where(
        step[None, :] < path_lengths[:, None], starts[:, None] + step[None, :], -1
    ).reshape(slots)
    row = jnp.arange(live)
    pick = place[None, :] == row[:, None]
    later = jnp.concatenate([pick[:, 1:], jnp.zeros((live, 1), bool)], axis=1)
    slot = jnp.arange(slots) % ACCEPT
    prev = ((slot < ACCEPT - 1)[None, :] & later & (slot >= 0)[None, :]) | (
        (slot == 0)[None, :] & pick
    )
    return pick, prev


def shards(
    queries,
    draft_node_keys,
    draft_node_values,
    prompt_keys,
    prompt_values,
    request_group,
    parents,
    node_visibility_mask,
    path_nodes,
    path_lengths,
    fc_node,
    fc_parent,
    norm_gain,
    w_gate,
    w_up,
    w_down,
):
    ctx_count = lax.axis_size("ctx")
    head_count = lax.axis_size("head")
    requests = request_group.shape[0]
    kv_heads = draft_node_keys.shape[1] // HEAD_SIZE
    width = queries.shape[1]
    repeat = width // HEAD_SIZE // kv_heads
    slots = requests * ACCEPT

    gathered = lax.all_gather(queries, "ctx", axis=0, tiled=True)

    mask = node_visibility_mask[0]
    chosen = (path_nodes[0][:, None] == jnp.arange(TREE_NODES)[None, :]).astype(BF16)
    path_queries = jnp.dot(chosen, queries, preferred_element_type=F32).astype(BF16)
    path_mask = jnp.dot(chosen, mask.astype(BF16), preferred_element_type=F32)
    pick, prev = live_rows(path_lengths)

    path_all = spread_all(path_queries, "ctx").reshape(slots, width)
    path_part = path_attend(path_all, prompt_keys, prompt_values, request_group, kv_heads, repeat)
    path_recv = swap(path_part.reshape(requests, ACCEPT, width + LANES), "ctx")
    features = combine(
        path_recv,
        path_queries,
        draft_node_keys,
        draft_node_values,
        path_mask,
        kv_heads,
        repeat,
        ctx_count,
        "path_combine",
    )
    every_row = swap(features, "ctx").reshape(slots, width)
    x_total = fc_project(every_row, pick.astype(BF16), prev.astype(BF16), fc_node, fc_parent)
    distance = 1
    x_other = jnp.zeros_like(x_total)
    while distance < head_count:
        if distance > 1:
            x_total = x_total + x_other
        x_other = partner(x_total, "head", distance)
        distance *= 2

    bulk_part = bulk_attend(
        gathered.reshape(requests, TREE_NODES, width),
        prompt_keys,
        prompt_values,
        request_group,
        kv_heads,
        repeat,
    )
    bulk_recv = swap(bulk_part, "ctx")
    attention_fn = combine(
        bulk_recv,
        queries,
        draft_node_keys,
        draft_node_values,
        mask.astype(F32),
        kv_heads,
        repeat,
        1,
        "bulk_combine",
    )[0]

    units = w_gate.shape[1] // ctx_count
    gain = norm_gain[None, :]
    if units % LANES == 0:
        partial = gate_up(x_total, x_other, gain, w_gate, w_up, ctx_count)
        hidden = activate(swap(partial, "ctx"))
        hidden_all = swap(hidden, "ctx")
    else:
        x = x_total + x_other
        scaled = (x * gain).astype(BF16)
        both = jnp.stack(
            [
                jnp.dot(scaled, w_gate, preferred_element_type=F32),
                jnp.dot(scaled, w_up, preferred_element_type=F32),
            ]
        )
        both = lax.psum_scatter(both, "ctx", scatter_dimension=2, tiled=True)
        squares = lax.psum(jnp.sum(x * x, axis=1), "ctx")
        both = both * lax.rsqrt(squares / MODEL_WIDTH + 1e-05)[None, :, None]
        hidden = (jax.nn.silu(both[0]) * both[1]).astype(BF16)
        hidden_all = lax.all_gather(hidden, "ctx", axis=1, tiled=True)[None]
    spread = pick.T.astype(F32)
    head = lax.axis_index("head").reshape(1)
    expanded = down_project(head, hidden_all, w_down, x_total, x_other, spread)
    pieces = swap(expanded.reshape(head_count, slots // head_count, -1), "head")
    draft_out = jnp.sum(pieces, axis=0).astype(BF16)
    return (attention_fn, draft_out)


def solution(mesh):
    return jax.shard_map(
        shards,
        mesh=mesh,
        in_specs=(
            P("ctx", "head"),
            P("ctx", "head"),
            P("ctx", "head"),
            P(None, "ctx", "head"),
            P(None, "ctx", "head"),
            P(),
            P("ctx", None),
            P("ctx", None, None),
            P("ctx", None),
            P(),
            P("head", "ctx"),
            P("head", "ctx"),
            P("ctx"),
            P("ctx", "head"),
            P("ctx", "head"),
            P("head", "ctx"),
        ),
        out_specs=(P("ctx", "head"), P("head", "ctx")),
        check_vma=False,
    )
```

```python
import functools

import jax
import jax.numpy as jnp
from jax import lax
from jax.experimental import pallas as pl
from jax.experimental.pallas import tpu as pltpu
from jax.sharding import PartitionSpec as P

MODEL_WIDTH = 8192
HEAD_SIZE = 128
TREE_NODES = 64
ACCEPT = 8
LANES = 128
LOG2E = 1.4426950408889634
SCORE_BASE2 = HEAD_SIZE ** (-0.5) * LOG2E

BULK_MIB = 60
BF16 = jnp.bfloat16
F32 = jnp.float32


def dot_nt(a, b):
    return lax.dot_general(a, b, (((1,), (1,)), ((), ())), preferred_element_type=F32)


def dot_nn(a, b):
    return lax.dot_general(a, b, (((1,), (0,)), ((), ())), preferred_element_type=F32)


def split_lanes(stat, width):
    hi = stat.astype(BF16).astype(F32)
    mid = (stat - hi).astype(BF16).astype(F32)
    lo = (stat - hi - mid).astype(BF16).astype(F32)
    packed = hi + pltpu.roll(mid, width, 1) + pltpu.roll(lo, 2 * width, 1)
    return packed.astype(BF16)


def join_lanes(packed, width):
    wide = packed.astype(F32)
    return (
        wide + pltpu.roll(wide, LANES - width, 1) + pltpu.roll(wide, LANES - 2 * width, 1)
    )


def vmem(limit_mib):
    return pltpu.CompilerParams(vmem_limit_bytes=limit_mib << 20)


def shard_rows(q_heads, score_fn, mix_fn):
    q = jnp.concatenate(q_heads, axis=0)
    raw = score_fn(q)
    top = jnp.max(raw, axis=1, keepdims=True) * SCORE_BASE2
    weights = jnp.exp2(raw * SCORE_BASE2 - top)
    total = jnp.sum(weights, axis=1, keepdims=True)
    out = (mix_fn(weights) / total).astype(BF16)
    return out, top + jnp.log(total) * LOG2E


def bulk_rows(q_ref, pairs, heads, step, finish):
    nodes = q_ref.shape[1]
    for first in range(0, heads, step):
        q = jnp.concatenate(
            [
                q_ref[0, :, h * HEAD_SIZE : (h + 1) * HEAD_SIZE]
                for h in range(first, first + step)
            ],
            axis=0,
        )
        raws = [dot_nt(q, keys) for keys, _ in pairs]
        tops = [jnp.max(raw, axis=1, keepdims=True) for raw in raws]
        top = functools.reduce(jnp.maximum, tops) * SCORE_BASE2
        total = 0.0
        mixed = 0.0
        for raw, (_, values) in zip(raws, pairs):
            weights = jnp.exp2(raw * SCORE_BASE2 - top)
            total += jnp.sum(weights, axis=1, keepdims=True)
            mixed += dot_nn(weights.astype(BF16), values)
        out = (mixed / total).astype(BF16)
        lse = top + jnp.log(total) * LOG2E
        for i in range(step):
            finish(first + i, out[i * nodes : (i + 1) * nodes], lse[i * nodes : (i + 1) * nodes])


def bulk_kernel(group_ref, place_ref, q_ref, *refs, repeat, outputs, step):
    blocks, outs, held = refs[: -outputs - 1], refs[-outputs - 1 : -1], refs[-1]
    nodes = q_ref.shape[1]
    turn = pl.program_id(0)
    group = group_ref[place_ref[0] ^ turn if outputs > 1 else turn]
    lane = lax.broadcasted_iota(jnp.int32, (nodes, LANES), 1)
    stat = [jnp.zeros((nodes, LANES), F32)]

    def finish(h, out, lse):
        held[:, h * HEAD_SIZE : (h + 1) * HEAD_SIZE] = out
        stat[0] = jnp.where(lane == h, lse, stat[0])

    pairs = [
        (blocks[i][group], blocks[i + 1][group]) for i in range(0, len(blocks), 2)
    ]
    bulk_rows(q_ref, pairs, repeat, step, finish)
    held[:, repeat * HEAD_SIZE :] = split_lanes(stat[0], repeat)
    if outputs == 1:
        outs[0][0] = held[...]
    for i in range(outputs):
        if outputs > 1:

            @pl.when(turn == i)
            def _(i=i):
                outs[i][...] = held[...]


def bulk_attend(queries, blocks, groups, place, repeat, ordered):
    requests, nodes, width = queries.shape
    out_width = width + LANES
    outputs = requests if ordered else 1
    work = requests * nodes * width * sum(block.shape[1] for block in blocks) // 2

    def query_map(r, g, c):
        return (c[0] ^ r if ordered else r, 0, 0)

    def block_map(wide):
        return lambda r, g, c: (0, 0, c[0] % 2 if wide else 0)

    specs = [
        pl.BlockSpec(
            block.shape[:2] + (HEAD_SIZE,),
            block_map(block.shape[2] > HEAD_SIZE),
            pipeline_mode=pl.Buffered(1),
        )
        for block in blocks
    ]
    if ordered:
        out_shape = [jax.ShapeDtypeStruct((nodes, out_width), BF16)] * requests
        out_specs = [pl.BlockSpec((nodes, out_width), lambda r, g, c: (0, 0))] * requests
    else:
        out_shape = [jax.ShapeDtypeStruct((requests, nodes, out_width), BF16)]
        out_specs = [pl.BlockSpec((1, nodes, out_width), lambda r, g, c: (r, 0, 0))]
    return pl.pallas_call(
        functools.partial(bulk_kernel, repeat=repeat, outputs=outputs, step=min(4, repeat)),
        out_shape=out_shape,
        grid_spec=pltpu.PrefetchScalarGridSpec(
            num_scalar_prefetch=2,
            grid=(requests,),
            in_specs=[pl.BlockSpec((1, nodes, width), query_map)] + specs,
            out_specs=out_specs,
            scratch_shapes=[pltpu.VMEM((nodes, out_width), BF16)],
        ),
        compiler_params=vmem(BULK_MIB),
        cost_estimate=pl.CostEstimate(
            flops=4 * work, bytes_accessed=8 << 20, transcendentals=work // HEAD_SIZE
        ),
        name="bulk_attend",
    )(groups, place, queries, *blocks)


def path_kernel(group_ref, q_ref, k_ref, v_ref, o_ref, *, kv_heads, repeat, step, per_block):
    rows_block = q_ref.shape[0]
    heads = kv_heads * repeat
    lane = lax.broadcasted_iota(jnp.int32, (rows_block, LANES), 1)
    owner = lax.broadcasted_iota(jnp.int32, (rows_block, 1), 0) // ACCEPT
    row_group = jnp.zeros((rows_block, 1), jnp.int32)
    for i in range(per_block):
        row_group = jnp.where(
            owner == i, group_ref[pl.program_id(0) * per_block + i], row_group
        )
    first_group = jnp.concatenate([row_group] * step, axis=0) == 0
    stat = jnp.zeros((rows_block, LANES), F32)
    for k in range(kv_heads):
        cols = slice(k * HEAD_SIZE, (k + 1) * HEAD_SIZE)
        for first in range(k * repeat, (k + 1) * repeat, step):
            out, lse = shard_rows(
                [
                    q_ref[:, h * HEAD_SIZE : (h + 1) * HEAD_SIZE]
                    for h in range(first, first + step)
                ],
                lambda q: jnp.where(
                    first_group, dot_nt(q, k_ref[0, :, cols]), dot_nt(q, k_ref[1, :, cols])
                ),
                lambda w: jnp.where(
                    first_group,
                    dot_nn(w.astype(BF16), v_ref[0, :, cols]),
                    dot_nn(w.astype(BF16), v_ref[1, :, cols]),
                ),
            )
            for i in range(step):
                h = first + i
                rows = slice(i * rows_block, (i + 1) * rows_block)
                o_ref[:, h * HEAD_SIZE : (h + 1) * HEAD_SIZE] = out[rows]
                stat = jnp.where(lane == h, lse[rows], stat)
    o_ref[:, heads * HEAD_SIZE :] = split_lanes(stat, heads)


def path_attend(rows_all, keys, values, groups, kv_heads, repeat):
    rows, width = rows_all.shape
    out_width = width + LANES
    per_block = 8
    block = per_block * ACCEPT
    work = rows * keys.shape[1] * width
    return pl.pallas_call(
        functools.partial(
            path_kernel,
            kv_heads=kv_heads,
            repeat=repeat,
            step=min(4, repeat),
            per_block=per_block,
        ),
        out_shape=jax.ShapeDtypeStruct((rows, out_width), BF16),
        grid_spec=pltpu.PrefetchScalarGridSpec(
            num_scalar_prefetch=1,
            grid=(rows // block,),
            in_specs=[
                pl.BlockSpec((block, width), lambda r, g: (r, 0)),
                pl.BlockSpec(keys.shape, lambda r, g: (0, 0, 0)),
                pl.BlockSpec(values.shape, lambda r, g: (0, 0, 0)),
            ],
            out_specs=pl.BlockSpec((block, out_width), lambda r, g: (r, 0)),
        ),
        compiler_params=vmem(60),
        cost_estimate=pl.CostEstimate(
            flops=8 * work, bytes_accessed=3 << 20, transcendentals=work // HEAD_SIZE
        ),
        name="path_attend",
    )(groups, rows_all, keys, values)


def merge_heads(parts, stats, base, q_ref, k_ref, v_ref, mask_ref, o_ref, repeat):
    rows = q_ref.shape[0]
    copies = o_ref.shape[0]
    best_src = functools.reduce(jnp.maximum, stats)
    q = jnp.concatenate(
        [q_ref[:, i * HEAD_SIZE : (i + 1) * HEAD_SIZE].astype(F32) for i in range(repeat)],
        axis=0,
    ).astype(BF16)
    allowed = jnp.concatenate([mask_ref[...]] * repeat, axis=0) > 0
    raw = jnp.where(allowed, dot_nt(q, k_ref[...]) * SCORE_BASE2, -1e30)
    top = jnp.max(raw, axis=1, keepdims=True)
    weights = jnp.where(allowed, jnp.exp2(raw - top), 0.0)
    total = jnp.sum(weights, axis=1, keepdims=True)
    mixed = dot_nn(weights.astype(BF16), v_ref[...])
    lane = lax.broadcasted_iota(jnp.int32, (rows, LANES), 1)
    for i in range(repeat):
        picked = lane == base + i
        own = slice(i * rows, (i + 1) * rows)

        def column(stat):
            return jnp.sum(jnp.where(picked, stat, 0.0), axis=1, keepdims=True)

        best = jnp.maximum(column(best_src), top[own])
        tree_scale = jnp.exp2(top[own] - best)
        numer = tree_scale * mixed[own]
        denom = tree_scale * total[own]
        for part, stat in zip(parts, stats):
            scale = jnp.exp2(column(stat) - best)
            numer += scale * part(i).astype(F32)
            denom += scale
        out = (numer / denom).astype(BF16)
        for j in range(copies):
            o_ref[j, :, i * HEAD_SIZE : (i + 1) * HEAD_SIZE] = out


def combine_kernel(recv_ref, stat_ref, q_ref, k_ref, v_ref, mask_ref, o_ref, *, repeat, heads):
    sources = recv_ref.shape[0]
    merge_heads(
        [
            lambda i, c=c: recv_ref[c, :, i * HEAD_SIZE : (i + 1) * HEAD_SIZE]
            for c in range(sources)
        ],
        [join_lanes(stat_ref[c], heads) for c in range(sources)],
        pl.program_id(0) * repeat,
        q_ref,
        k_ref,
        v_ref,
        mask_ref,
        o_ref,
        repeat,
    )


def combine(recv, queries, tree_keys, tree_values, mask, kv_heads, repeat, copies, name):
    sources, rows, wide = recv.shape
    width = wide - LANES
    part = repeat * HEAD_SIZE
    return pl.pallas_call(
        functools.partial(combine_kernel, repeat=repeat, heads=kv_heads * repeat),
        out_shape=jax.ShapeDtypeStruct((copies, rows, width), BF16),
        grid=(kv_heads,),
        in_specs=[
            pl.BlockSpec((sources, rows, part), lambda k: (0, 0, k)),
            pl.BlockSpec((sources, rows, LANES), lambda k: (0, 0, width // LANES)),
            pl.BlockSpec((rows, part), lambda k: (0, k)),
            pl.BlockSpec((TREE_NODES, HEAD_SIZE), lambda k: (0, k)),
            pl.BlockSpec((TREE_NODES, HEAD_SIZE), lambda k: (0, k)),
            pl.BlockSpec((rows, TREE_NODES), lambda k: (0, 0)),
        ],
        out_specs=pl.BlockSpec((copies, rows, part), lambda k: (0, 0, k)),
        compiler_params=vmem(60),
        cost_estimate=pl.CostEstimate(
            flops=4 * rows * width * TREE_NODES,
            bytes_accessed=2 * recv.size + 4 * rows * width,
            transcendentals=rows * width // 2,
        ),
        name=name,
    )(recv, recv, queries, tree_keys, tree_values, mask)


def pair_kernel(place_ref, *refs, repeat):
    sources, rest = refs[:-5], refs[-5:]
    q_ref, k_ref, v_ref, mask_ref, o_ref = rest
    part = repeat * HEAD_SIZE
    for turn in range(2):

        @pl.when(pl.program_id(0) == turn)
        def _(turn=turn):
            mine = sources[turn::2]
            merge_heads(
                [
                    lambda i, ref=ref: ref[:, i * HEAD_SIZE : (i + 1) * HEAD_SIZE]
                    for ref in mine
                ],
                [join_lanes(ref[:, part:], repeat) for ref in mine],
                0,
                q_ref,
                k_ref,
                v_ref,
                mask_ref,
                o_ref,
                repeat,
            )


def combine_pair(place, sources, queries, tree_keys, tree_values, mask, repeat):
    rows, width = queries.shape
    part = repeat * HEAD_SIZE

    def head(j, p):
        return (0, p[0] % 2 ^ j)

    return pl.pallas_call(
        functools.partial(pair_kernel, repeat=repeat),
        out_shape=jax.ShapeDtypeStruct((1, rows, width), BF16),
        grid_spec=pltpu.PrefetchScalarGridSpec(
            num_scalar_prefetch=1,
            grid=(2,),
            in_specs=[pl.BlockSpec(source.shape, lambda j, p: (0, 0)) for source in sources]
            + [
                pl.BlockSpec((rows, part), head),
                pl.BlockSpec((TREE_NODES, HEAD_SIZE), head),
                pl.BlockSpec((TREE_NODES, HEAD_SIZE), head),
                pl.BlockSpec((rows, TREE_NODES), lambda j, p: (0, 0)),
            ],
            out_specs=pl.BlockSpec((1, rows, part), lambda j, p: (0, 0, p[0] % 2 ^ j)),
        ),
        compiler_params=vmem(60),
        cost_estimate=pl.CostEstimate(
            flops=4 * rows * width * TREE_NODES,
            bytes_accessed=12 * rows * width,
            transcendentals=rows * width // 2,
        ),
        name="combine_pair",
    )(place, *sources, queries, tree_keys, tree_values, mask)


def fc_kernel(feat_ref, pick_ref, prev_ref, wn_ref, wp_ref, o_ref):
    feats = feat_ref[...]
    node = dot_nn(pick_ref[...], feats).astype(BF16)
    parent = dot_nn(prev_ref[...], feats).astype(BF16)
    part = dot_nn(node, wn_ref[...]) + dot_nn(parent, wp_ref[...])

    @pl.when(pl.program_id(0) == 0)
    def _():
        o_ref[...] = part

    @pl.when(pl.program_id(0) > 0)
    def _():
        o_ref[...] += part


def fc_project(feats, pick, prev, fc_node, fc_parent):
    slots, width = feats.shape
    live = pick.shape[0]
    cols = fc_node.shape[1]
    block = min(width, 512)
    return pl.pallas_call(
        fc_kernel,
        out_shape=jax.ShapeDtypeStruct((live, cols), F32),
        grid=(width // block,),
        in_specs=[
            pl.BlockSpec((slots, block), lambda i: (0, i)),
            pl.BlockSpec((live, slots), lambda i: (0, 0)),
            pl.BlockSpec((live, slots), lambda i: (0, 0)),
            pl.BlockSpec((block, cols), lambda i: (i, 0)),
            pl.BlockSpec((block, cols), lambda i: (i, 0)),
        ],
        out_specs=pl.BlockSpec((live, cols), lambda i: (0, 0)),
        compiler_params=vmem(60),
        cost_estimate=pl.CostEstimate(
            flops=4 * live * width * cols, bytes_accessed=4 * width * cols, transcendentals=0
        ),
        name="fc_project",
    )(feats, pick, prev, fc_node, fc_parent)


def gate_kernel(xa_ref, xb_ref, gain_ref, wg_ref, wu_ref, o_ref):
    x = xa_ref[...] + xb_ref[...]
    units = wg_ref.shape[1]
    scaled = (x * gain_ref[...]).astype(BF16)
    o_ref[0, :, :units] = dot_nn(scaled, wg_ref[...]).astype(BF16)
    o_ref[0, :, units : 2 * units] = dot_nn(scaled, wu_ref[...]).astype(BF16)
    squares = jnp.sum(x * x, axis=1, keepdims=True)
    lane = lax.broadcasted_iota(jnp.int32, (x.shape[0], LANES), 1)
    o_ref[0, :, 2 * units :] = split_lanes(jnp.where(lane == 0, squares, 0.0), 1)


def gate_up(xa, xb, gain, w_gate, w_up, parts):
    live, width = xa.shape
    units = w_gate.shape[1] // parts
    return pl.pallas_call(
        gate_kernel,
        out_shape=jax.ShapeDtypeStruct((parts, live, 2 * units + LANES), BF16),
        grid=(parts,),
        in_specs=[
            pl.BlockSpec((live, width), lambda i: (0, 0)),
            pl.BlockSpec((live, width), lambda i: (0, 0)),
            pl.BlockSpec((1, width), lambda i: (0, 0)),
            pl.BlockSpec((width, units), lambda i: (0, i)),
            pl.BlockSpec((width, units), lambda i: (0, i)),
        ],
        out_specs=pl.BlockSpec((1, live, 2 * units + LANES), lambda i: (i, 0, 0)),
        compiler_params=vmem(60),
        cost_estimate=pl.CostEstimate(
            flops=4 * live * width * units * parts,
            bytes_accessed=4 * width * units * parts,
            transcendentals=0,
        ),
        name="gate_up",
    )(xa, xb, gain, w_gate, w_up)


def act_kernel(recv_ref, o_ref):
    units = o_ref.shape[2]
    sources = recv_ref.shape[0]
    total = recv_ref[0].astype(F32)
    for c in range(1, sources):
        total += recv_ref[c].astype(F32)
    squares = jnp.sum(total[:, 2 * units :], axis=1, keepdims=True)
    scale = lax.rsqrt(squares / MODEL_WIDTH + 1e-05)
    gate = total[:, :units] * scale
    up = total[:, units : 2 * units] * scale
    hidden = (gate / (1.0 + jnp.exp(-gate)) * up).astype(BF16)
    for c in range(sources):
        o_ref[c] = hidden


def activate(recv):
    sources, live, wide = recv.shape
    units = (wide - LANES) // 2
    return pl.pallas_call(
        act_kernel,
        out_shape=jax.ShapeDtypeStruct((sources, live, units), BF16),
        compiler_params=vmem(60),
        cost_estimate=pl.CostEstimate(
            flops=recv.size, bytes_accessed=3 * recv.size, transcendentals=live * units
        ),
        name="activate",
    )(recv)


def down_kernel(head_ref, hid_ref, w_ref, xa_ref, xb_ref, spread_ref, o_ref, acc_ref):
    @pl.when(pl.program_id(0) == 0)
    def _():
        residual = xa_ref[...] + xb_ref[...]
        acc_ref[...] = jnp.where(head_ref[0] == 0, residual, 0.0)

    acc_ref[...] += dot_nn(hid_ref[0], w_ref[...])

    @pl.when(pl.program_id(0) == pl.num_programs(0) - 1)
    def _():
        o_ref[...] = lax.dot_general(
            spread_ref[...],
            acc_ref[...],
            (((1,), (0,)), ((), ())),
            precision=lax.Precision.HIGHEST,
            preferred_element_type=F32,
        )


def down_project(head, hidden, w_down, xa, xb, spread):
    parts, live, units = hidden.shape
    cols = w_down.shape[1]
    slots = spread.shape[0]
    return pl.pallas_call(
        down_kernel,
        out_shape=jax.ShapeDtypeStruct((slots, cols), F32),
        grid_spec=pltpu.PrefetchScalarGridSpec(
            num_scalar_prefetch=1,
            grid=(parts,),
            in_specs=[
                pl.BlockSpec((1, live, units), lambda i, h: (i, 0, 0)),
                pl.BlockSpec((units, cols), lambda i, h: (i, 0)),
                pl.BlockSpec((live, cols), lambda i, h: (0, 0)),
                pl.BlockSpec((live, cols), lambda i, h: (0, 0)),
                pl.BlockSpec((slots, live), lambda i, h: (0, 0)),
            ],
            out_specs=pl.BlockSpec((slots, cols), lambda i, h: (0, 0)),
            scratch_shapes=[pltpu.VMEM((live, cols), F32)],
        ),
        compiler_params=vmem(60),
        cost_estimate=pl.CostEstimate(
            flops=2 * live * parts * units * cols,
            bytes_accessed=2 * parts * units * cols,
            transcendentals=0,
        ),
        name="down_project",
    )(head, hidden, w_down, xa, xb, spread)


def swap(blocks, axis):
    return lax.all_to_all(blocks, axis, split_axis=0, concat_axis=0, tiled=True)


def spread_all(block, axis):
    count = lax.axis_size(axis)
    return swap(jnp.broadcast_to(block[None], (count,) + block.shape), axis)


def partner(value, axis, distance):
    count = lax.axis_size(axis)
    return lax.ppermute(value, axis, [(i, i ^ distance) for i in range(count)])


def live_rows(path_lengths):
    requests = path_lengths.shape[0]
    slots = requests * ACCEPT
    live = slots // 2
    index = jnp.arange(requests)
    starts = jnp.sum(
        jnp.where(index[None, :] < index[:, None], path_lengths[None, :], 0), axis=1
    )
    step = jnp.arange(ACCEPT)
    place = jnp.where(
        step[None, :] < path_lengths[:, None], starts[:, None] + step[None, :], -1
    ).reshape(slots)
    row = jnp.arange(live)
    pick = place[None, :] == row[:, None]
    later = jnp.concatenate([pick[:, 1:], jnp.zeros((live, 1), bool)], axis=1)
    slot = jnp.arange(slots) % ACCEPT
    prev = ((slot < ACCEPT - 1)[None, :] & later & (slot >= 0)[None, :]) | (
        (slot == 0)[None, :] & pick
    )
    return pick, prev


def shards(
    queries,
    draft_node_keys,
    draft_node_values,
    prompt_keys,
    prompt_values,
    request_group,
    parents,
    node_visibility_mask,
    path_nodes,
    path_lengths,
    fc_node,
    fc_parent,
    norm_gain,
    w_gate,
    w_up,
    w_down,
):
    ctx_count = lax.axis_size("ctx")
    head_count = lax.axis_size("head")
    requests = request_group.shape[0]
    kv_heads = draft_node_keys.shape[1] // HEAD_SIZE
    width = queries.shape[1]
    repeat = width // HEAD_SIZE // kv_heads
    slots = requests * ACCEPT

    paired = kv_heads == 2 and ctx_count % 2 == 0
    me = lax.axis_index("ctx")
    place = me.reshape(1)
    paired = paired and requests == ctx_count and ctx_count & (ctx_count - 1) == 0
    if paired:
        part = repeat * HEAD_SIZE
        halves = jnp.stack([queries[:, :part], queries[:, part:]])
        outgoing = jnp.broadcast_to(
            halves[None], (ctx_count // 2,) + halves.shape
        ).reshape(ctx_count, TREE_NODES, part)
    else:
        outgoing = None

    mask = node_visibility_mask[0]
    chosen = (path_nodes[0][:, None] == jnp.arange(TREE_NODES)[None, :]).astype(BF16)
    path_queries = jnp.dot(chosen, queries, preferred_element_type=F32).astype(BF16)
    path_mask = jnp.dot(chosen, mask.astype(BF16), preferred_element_type=F32)
    pick, prev = live_rows(path_lengths)

    path_all = spread_all(path_queries, "ctx").reshape(slots, width)
    path_part = path_attend(path_all, prompt_keys, prompt_values, request_group, kv_heads, repeat)
    path_recv = swap(path_part.reshape(requests, ACCEPT, width + LANES), "ctx")
    features = combine(
        path_recv,
        path_queries,
        draft_node_keys,
        draft_node_values,
        path_mask,
        kv_heads,
        repeat,
        ctx_count,
        "path_combine",
    )
    every_row = swap(features, "ctx").reshape(slots, width)
    if paired:
        other = (1 - me % 2) * HEAD_SIZE
        far_keys = partner(lax.dynamic_slice_in_dim(prompt_keys, other, HEAD_SIZE, 2), "ctx", 1)
        far_values = partner(lax.dynamic_slice_in_dim(prompt_values, other, HEAD_SIZE, 2), "ctx", 1)
        every_row, far_keys, far_values, outgoing = lax.optimization_barrier(
            (every_row, far_keys, far_values, outgoing)
        )
        blocks = [prompt_keys, prompt_values, far_keys, far_values]
        bulk_queries = swap(outgoing, "ctx")
    else:
        blocks = [prompt_keys, prompt_values]
        bulk_queries = lax.all_gather(queries, "ctx", axis=0)

    x_total = fc_project(every_row, pick.astype(BF16), prev.astype(BF16), fc_node, fc_parent)
    distance = 1
    x_other = jnp.zeros_like(x_total)
    while distance < head_count:
        if distance > 1:
            x_total = x_total + x_other
        x_other = partner(x_total, "head", distance)
        distance *= 2

    units = w_gate.shape[1] // ctx_count
    gain = norm_gain[None, :]
    by_lanes = units % LANES == 0
    if by_lanes:
        partial = gate_up(x_total, x_other, gain, w_gate, w_up, ctx_count)
        if paired:
            partial, bulk_queries = lax.optimization_barrier((partial, bulk_queries))
        summed = swap(partial, "ctx")
    else:
        x = x_total + x_other
        scaled = (x * gain).astype(BF16)
        both = jnp.stack(
            [
                jnp.dot(scaled, w_gate, preferred_element_type=F32),
                jnp.dot(scaled, w_up, preferred_element_type=F32),
            ]
        )
        both = lax.psum_scatter(both, "ctx", scatter_dimension=2, tiled=True)
        squares = lax.psum(jnp.sum(x * x, axis=1), "ctx")
        summed = both * lax.rsqrt(squares / MODEL_WIDTH + 1e-05)[None, :, None]

    if paired:
        bulk_part = bulk_attend(bulk_queries, blocks, request_group, place, repeat, True)
        summed, bulk_part = lax.optimization_barrier((summed, bulk_part))
        sources = [bulk_part[0]] + [
            partner(bulk_part[i], "ctx", i) for i in range(1, ctx_count)
        ]
        attention_fn = combine_pair(
            place,
            sources,
            queries,
            draft_node_keys,
            draft_node_values,
            mask.astype(F32),
            repeat,
        )[0]
    else:
        parts = []
        for k in range(kv_heads):
            cols = slice(k * HEAD_SIZE, (k + 1) * HEAD_SIZE)
            heads = slice(k * repeat * HEAD_SIZE, (k + 1) * repeat * HEAD_SIZE)
            (part,) = bulk_attend(
                bulk_queries[:, :, heads],
                [block[:, :, cols] for block in blocks],
                request_group,
                place,
                repeat,
                False,
            )
            parts.append(
                combine(
                    swap(part, "ctx"),
                    queries[:, heads],
                    draft_node_keys[:, cols],
                    draft_node_values[:, cols],
                    mask.astype(F32),
                    1,
                    repeat,
                    1,
                    "bulk_combine",
                )[0]
            )
        attention_fn = jnp.concatenate(parts, axis=1)

    if by_lanes:
        hidden_all = swap(activate(summed), "ctx")
    else:
        hidden = (jax.nn.silu(summed[0]) * summed[1]).astype(BF16)
        hidden_all = lax.all_gather(hidden, "ctx", axis=1, tiled=True)[None]
    spread = pick.T.astype(F32)
    head = lax.axis_index("head").reshape(1)
    expanded = down_project(head, hidden_all, w_down, x_total, x_other, spread)
    pieces = swap(expanded.reshape(head_count, slots // head_count, -1), "head")
    draft_out = jnp.sum(pieces, axis=0).astype(BF16)
    return (attention_fn, draft_out)


def solution(mesh):
    return jax.shard_map(
        shards,
        mesh=mesh,
        in_specs=(
            P("ctx", "head"),
            P("ctx", "head"),
            P("ctx", "head"),
            P(None, "ctx", "head"),
            P(None, "ctx", "head"),
            P(),
            P("ctx", None),
            P("ctx", None, None),
            P("ctx", None),
            P(),
            P("head", "ctx"),
            P("head", "ctx"),
            P("ctx"),
            P("ctx", "head"),
            P("ctx", "head"),
            P("head", "ctx"),
        ),
        out_specs=(P("ctx", "head"), P("head", "ctx")),
        check_vma=False,
    )
```

```python
import functools

import jax
import jax.numpy as jnp
from jax import lax
from jax.experimental import pallas as pl
from jax.experimental.pallas import tpu as pltpu
from jax.sharding import PartitionSpec as P

MODEL_WIDTH = 8192
HEAD_SIZE = 128
TREE_NODES = 64
ACCEPT = 8
LANES = 128
LOG2E = 1.4426950408889634
SCORE_BASE2 = HEAD_SIZE ** (-0.5) * LOG2E

VMEM_MIB = 64
BF16 = jnp.bfloat16
F32 = jnp.float32


def dot_nt(a, b):
    return lax.dot_general(a, b, (((1,), (1,)), ((), ())), preferred_element_type=F32)


def dot_nn(a, b):
    return lax.dot_general(a, b, (((1,), (0,)), ((), ())), preferred_element_type=F32)


def split_lanes(stat, width):
    hi = stat.astype(BF16).astype(F32)
    mid = (stat - hi).astype(BF16).astype(F32)
    lo = (stat - hi - mid).astype(BF16).astype(F32)
    packed = hi + pltpu.roll(mid, width, 1) + pltpu.roll(lo, 2 * width, 1)
    return packed.astype(BF16)


def join_lanes(packed, width):
    wide = packed.astype(F32)
    return (
        wide + pltpu.roll(wide, LANES - width, 1) + pltpu.roll(wide, LANES - 2 * width, 1)
    )


def vmem(limit_mib):
    return pltpu.CompilerParams(vmem_limit_bytes=limit_mib << 20)


def one_hot_rows(node_ref, rows):
    row = lax.broadcasted_iota(jnp.int32, (rows, TREE_NODES), 0)
    lane = lax.broadcasted_iota(jnp.int32, (rows, TREE_NODES), 1)
    node = jnp.zeros((rows, TREE_NODES), jnp.int32)
    for i in range(rows):
        node = jnp.where(row == i, node_ref[0, i], node)
    return (lane == node).astype(F32).astype(BF16)


def live_places(length_ref, requests, shape, axis):
    slot = lax.broadcasted_iota(jnp.int32, shape, axis)
    owner, step = slot // ACCEPT, slot % ACCEPT
    place = jnp.full(shape, -1, jnp.int32)
    child = jnp.full(shape, -1, jnp.int32)
    start = jnp.int32(0)
    for r in range(requests):
        length = length_ref[r]
        mine = owner == r
        place = jnp.where(mine & (step < length), start + step, place)
        child = jnp.where(mine & (step + 1 < length), start + step + 1, child)
        start = start + length
    return place, child, step


def query_kernel(node_ref, q_ref, all_ref, own_ref):
    rows = own_ref.shape[0]
    picked = dot_nn(one_hot_rows(node_ref, rows), q_ref[...]).astype(BF16)
    own_ref[...] = picked
    for c in range(all_ref.shape[0]):
        all_ref[c] = picked


def path_rows(path_nodes, queries, copies):
    width = queries.shape[1]
    return pl.pallas_call(
        query_kernel,
        out_shape=[
            jax.ShapeDtypeStruct((copies, ACCEPT, width), BF16),
            jax.ShapeDtypeStruct((ACCEPT, width), BF16),
        ],
        in_specs=[
            pl.BlockSpec(memory_space=pltpu.SMEM),
            pl.BlockSpec(memory_space=pltpu.VMEM),
        ],
        compiler_params=vmem(VMEM_MIB),
        name="path_rows",
    )(path_nodes, queries)


def shard_rows(q_heads, score_fn, mix_fn):
    q = jnp.concatenate(q_heads, axis=0)
    raw = score_fn(q)
    top = jnp.max(raw, axis=1, keepdims=True) * SCORE_BASE2
    weights = jnp.exp2(raw * SCORE_BASE2 - top)
    total = jnp.sum(weights, axis=1, keepdims=True)
    out = (mix_fn(weights) / total).astype(BF16)
    return out, top + jnp.log(total) * LOG2E


def bulk_rows(q_ref, pairs, heads, step, finish):
    nodes = q_ref.shape[1]
    for first in range(0, heads, step):
        q = jnp.concatenate(
            [
                q_ref[0, :, h * HEAD_SIZE : (h + 1) * HEAD_SIZE]
                for h in range(first, first + step)
            ],
            axis=0,
        )
        raws = [dot_nt(q, keys) for keys, _ in pairs]
        tops = [jnp.max(raw, axis=1, keepdims=True) for raw in raws]
        top = functools.reduce(jnp.maximum, tops) * SCORE_BASE2
        total = 0.0
        mixed = 0.0
        for raw, (_, values) in zip(raws, pairs):
            weights = jnp.exp2(raw * SCORE_BASE2 - top)
            total += jnp.sum(weights, axis=1, keepdims=True)
            mixed += dot_nn(weights.astype(BF16), values)
        out = (mixed / total).astype(BF16)
        lse = top + jnp.log(total) * LOG2E
        for i in range(step):
            finish(first + i, out[i * nodes : (i + 1) * nodes], lse[i * nodes : (i + 1) * nodes])


def bulk_kernel(group_ref, place_ref, q_ref, *refs, repeat, which, step):
    blocks, o_ref = refs[:-1], refs[-1]
    nodes = q_ref.shape[1]
    group = group_ref[which(pl.program_id(0), place_ref[0])]
    lane = lax.broadcasted_iota(jnp.int32, (nodes, LANES), 1)
    stat = [jnp.zeros((nodes, LANES), F32)]

    def finish(h, out, lse):
        o_ref[0, :, h * HEAD_SIZE : (h + 1) * HEAD_SIZE] = out
        stat[0] = jnp.where(lane == h, lse, stat[0])

    pairs = [
        (blocks[i][group], blocks[i + 1][group]) for i in range(0, len(blocks), 2)
    ]
    bulk_rows(q_ref, pairs, repeat, step, finish)
    o_ref[0, :, repeat * HEAD_SIZE :] = split_lanes(stat[0], repeat)


def bulk_attend(queries, blocks, groups, place, repeat, odd):
    requests, nodes, width = queries.shape
    turns = requests if odd is None else requests // 2
    out_width = width + LANES
    work = turns * nodes * width * sum(block.shape[1] for block in blocks) // 2

    def which(turn, here):
        if odd is None:
            return turn
        return here ^ (turn // 2 * 4 + odd * 2 + turn % 2)

    def block_map(wide):
        return lambda r, g, c: (0, 0, c[0] % 2 if wide else 0)

    specs = [
        pl.BlockSpec(
            block.shape[:2] + (HEAD_SIZE,),
            block_map(block.shape[2] > HEAD_SIZE),
            pipeline_mode=pl.Buffered(1),
        )
        for block in blocks
    ]
    return pl.pallas_call(
        functools.partial(bulk_kernel, repeat=repeat, which=which, step=min(4, repeat)),
        out_shape=jax.ShapeDtypeStruct((turns, nodes, out_width), BF16),
        grid_spec=pltpu.PrefetchScalarGridSpec(
            num_scalar_prefetch=2,
            grid=(turns,),
            in_specs=[pl.BlockSpec((1, nodes, width), lambda r, g, c: (which(r, c[0]), 0, 0))]
            + specs,
            out_specs=pl.BlockSpec((1, nodes, out_width), lambda r, g, c: (r, 0, 0)),
        ),
        compiler_params=vmem(VMEM_MIB),
        cost_estimate=pl.CostEstimate(
            flops=4 * work, bytes_accessed=8 << 20, transcendentals=work // HEAD_SIZE
        ),
        name="bulk_attend",
    )(groups, place, queries, *blocks)


def path_kernel(group_ref, place_ref, q_ref, k_ref, v_ref, o_ref, *refs, kv_heads, repeat, step, per_block):
    traded, stat_ref = refs[:-1], refs[-1]
    rows_block = q_ref.shape[0]
    heads = kv_heads * repeat
    lane = lax.broadcasted_iota(jnp.int32, (rows_block, LANES), 1)
    owner = lax.broadcasted_iota(jnp.int32, (rows_block, 1), 0) // ACCEPT
    row_group = jnp.zeros((rows_block, 1), jnp.int32)
    for i in range(per_block):
        row_group = jnp.where(
            owner == i, group_ref[pl.program_id(0) * per_block + i], row_group
        )
    first_group = jnp.concatenate([row_group] * step, axis=0) == 0
    k = pl.program_id(1)
    if traded:

        @pl.when(k != place_ref[0] % 2)
        def _():
            traded[0][...] = k_ref[...]
            traded[1][...] = v_ref[...]

    @pl.when(k == 0)
    def _():
        stat_ref[...] = jnp.zeros_like(stat_ref)

    stat = stat_ref[...]
    for first in range(0, repeat, step):
        out, lse = shard_rows(
            [
                q_ref[:, h * HEAD_SIZE : (h + 1) * HEAD_SIZE]
                for h in range(first, first + step)
            ],
            lambda q: jnp.where(first_group, dot_nt(q, k_ref[0]), dot_nt(q, k_ref[1])),
            lambda w: jnp.where(
                first_group,
                dot_nn(w.astype(BF16), v_ref[0]),
                dot_nn(w.astype(BF16), v_ref[1]),
            ),
        )
        for i in range(step):
            h = k * repeat + first + i
            rows = slice(i * rows_block, (i + 1) * rows_block)
            cols = pl.ds(pl.multiple_of(h * HEAD_SIZE, HEAD_SIZE), HEAD_SIZE)
            o_ref[:, cols] = out[rows]
            stat = jnp.where(lane == h, lse[rows], stat)
    stat_ref[...] = stat

    @pl.when(k == kv_heads - 1)
    def _():
        o_ref[:, heads * HEAD_SIZE :] = split_lanes(stat, heads)


def path_attend(rows_all, keys, values, groups, place, kv_heads, repeat, trade):
    rows, width = rows_all.shape
    out_width = width + LANES
    per_block = 8
    block = per_block * ACCEPT
    moved = jax.ShapeDtypeStruct(keys.shape[:2] + (HEAD_SIZE,), BF16)
    work = rows * keys.shape[1] * width
    return pl.pallas_call(
        functools.partial(
            path_kernel,
            kv_heads=kv_heads,
            repeat=repeat,
            step=min(4, repeat),
            per_block=per_block,
        ),
        out_shape=[jax.ShapeDtypeStruct((rows, out_width), BF16)] + [moved] * (2 * trade),
        grid_spec=pltpu.PrefetchScalarGridSpec(
            num_scalar_prefetch=2,
            grid=(rows // block, kv_heads),
            in_specs=[
                pl.BlockSpec((block, width // kv_heads), lambda r, k, g, p: (r, k)),
                pl.BlockSpec(keys.shape[:2] + (HEAD_SIZE,), lambda r, k, g, p: (0, 0, k)),
                pl.BlockSpec(values.shape[:2] + (HEAD_SIZE,), lambda r, k, g, p: (0, 0, k)),
            ],
            out_specs=[pl.BlockSpec((block, out_width), lambda r, k, g, p: (r, 0))]
            + [pl.BlockSpec(moved.shape, lambda r, k, g, p: (0, 0, 0))] * (2 * trade),
            scratch_shapes=[pltpu.VMEM((block, LANES), F32)],
        ),
        compiler_params=vmem(VMEM_MIB),
        cost_estimate=pl.CostEstimate(
            flops=8 * work, bytes_accessed=3 << 20, transcendentals=work // HEAD_SIZE
        ),
        name="path_attend",
    )(groups, place, rows_all, keys, values)


def merge_heads(parts, stats, base, q_ref, k_ref, v_ref, mask, o_ref, repeat):
    rows = q_ref.shape[0]
    copies = o_ref.shape[0]
    best_src = functools.reduce(jnp.maximum, stats)
    q = jnp.concatenate(
        [q_ref[:, i * HEAD_SIZE : (i + 1) * HEAD_SIZE].astype(F32) for i in range(repeat)],
        axis=0,
    ).astype(BF16)
    allowed = jnp.concatenate([mask] * repeat, axis=0) > 0
    raw = jnp.where(allowed, dot_nt(q, k_ref[...]) * SCORE_BASE2, -1e30)
    top = jnp.max(raw, axis=1, keepdims=True)
    weights = jnp.where(allowed, jnp.exp2(raw - top), 0.0)
    total = jnp.sum(weights, axis=1, keepdims=True)
    mixed = dot_nn(weights.astype(BF16), v_ref[...])
    lane = lax.broadcasted_iota(jnp.int32, (rows, LANES), 1)
    for i in range(repeat):
        picked = lane == base + i
        own = slice(i * rows, (i + 1) * rows)

        def column(stat):
            return jnp.sum(jnp.where(picked, stat, 0.0), axis=1, keepdims=True)

        best = jnp.maximum(column(best_src), top[own])
        tree_scale = jnp.exp2(top[own] - best)
        numer = tree_scale * mixed[own]
        denom = tree_scale * total[own]
        for part, stat in zip(parts, stats):
            scale = jnp.exp2(column(stat) - best)
            numer += scale * part(i).astype(F32)
            denom += scale
        out = (numer / denom).astype(BF16)
        for j in range(copies):
            o_ref[j, :, i * HEAD_SIZE : (i + 1) * HEAD_SIZE] = out


def combine_kernel(
    node_ref, recv_ref, stat_ref, q_ref, k_ref, v_ref, mask_ref, o_ref, *, repeat, heads
):
    sources, rows, _ = recv_ref.shape
    mask = mask_ref[...].astype(F32)
    if rows < TREE_NODES:
        mask = dot_nn(one_hot_rows(node_ref, rows), mask.astype(BF16))
    merge_heads(
        [
            lambda i, c=c: recv_ref[c, :, i * HEAD_SIZE : (i + 1) * HEAD_SIZE]
            for c in range(sources)
        ],
        [join_lanes(stat_ref[c], heads) for c in range(sources)],
        pl.program_id(0) * repeat,
        q_ref,
        k_ref,
        v_ref,
        mask,
        o_ref,
        repeat,
    )


def combine(path_nodes, recv, queries, tree_keys, tree_values, mask, kv_heads, repeat, copies, name):
    sources, rows, wide = recv.shape
    width = wide - LANES
    part = repeat * HEAD_SIZE
    return pl.pallas_call(
        functools.partial(combine_kernel, repeat=repeat, heads=kv_heads * repeat),
        out_shape=jax.ShapeDtypeStruct((copies, rows, width), BF16),
        grid=(kv_heads,),
        in_specs=[
            pl.BlockSpec(memory_space=pltpu.SMEM),
            pl.BlockSpec((sources, rows, part), lambda k: (0, 0, k)),
            pl.BlockSpec((sources, rows, LANES), lambda k: (0, 0, width // LANES)),
            pl.BlockSpec((rows, part), lambda k: (0, k)),
            pl.BlockSpec((TREE_NODES, HEAD_SIZE), lambda k: (0, k)),
            pl.BlockSpec((TREE_NODES, HEAD_SIZE), lambda k: (0, k)),
            pl.BlockSpec((TREE_NODES, TREE_NODES), lambda k: (0, 0)),
        ],
        out_specs=pl.BlockSpec((copies, rows, part), lambda k: (0, 0, k)),
        compiler_params=vmem(VMEM_MIB),
        cost_estimate=pl.CostEstimate(
            flops=4 * rows * width * TREE_NODES,
            bytes_accessed=2 * recv.size + 4 * rows * width,
            transcendentals=rows * width // 2,
        ),
        name=name,
    )(path_nodes, recv, recv, queries, tree_keys, tree_values, mask)


def fold_kernel(*refs, repeat):
    sources, o_ref = refs[:-1], refs[-1]
    rows = o_ref.shape[1]
    part = repeat * HEAD_SIZE
    lane = lax.broadcasted_iota(jnp.int32, (rows, LANES), 1)
    stats = [join_lanes(ref[0, :, part:], repeat) for ref in sources]
    best = functools.reduce(jnp.maximum, stats)
    scales = [jnp.exp2(stat - best) for stat in stats]
    total = functools.reduce(jnp.add, scales)
    for i in range(repeat):
        cols = slice(i * HEAD_SIZE, (i + 1) * HEAD_SIZE)

        def column(stat):
            return jnp.sum(jnp.where(lane == i, stat, 0.0), axis=1, keepdims=True)

        numer = 0.0
        for ref, scale in zip(sources, scales):
            numer += column(scale) * ref[0, :, cols].astype(F32)
        o_ref[0, :, cols] = (numer / column(total)).astype(BF16)
    lse = best + jnp.log(total) * LOG2E
    o_ref[0, :, part:] = split_lanes(jnp.where(lane < repeat, lse, 0.0), repeat)


def fold_blocks(sources, first, count, repeat):
    _, rows, wide = sources[0].shape
    return pl.pallas_call(
        functools.partial(fold_kernel, repeat=repeat),
        out_shape=jax.ShapeDtypeStruct((count, rows, wide), BF16),
        grid=(count,),
        in_specs=[
            pl.BlockSpec((1, rows, wide), lambda j: (first + 2 * j, 0, 0)) for _ in sources
        ],
        out_specs=pl.BlockSpec((1, rows, wide), lambda j: (j, 0, 0)),
        compiler_params=vmem(VMEM_MIB),
        cost_estimate=pl.CostEstimate(
            flops=rows * wide, bytes_accessed=6 * rows * wide, transcendentals=0
        ),
        name="fold_blocks",
    )(*sources)


def pair_kernel(place_ref, *refs, repeat):
    count = (len(refs) - 5) // 2
    near, far, rest = refs[:count], refs[count:-5], refs[-5:]
    q_ref, k_ref, v_ref, mask_ref, o_ref = rest
    part = repeat * HEAD_SIZE
    for turn in range(2):

        @pl.when(pl.program_id(0) == turn)
        def _(turn=turn):
            mine = [ref.at[0] for ref in (near if turn == 0 else far)]
            merge_heads(
                [
                    lambda i, ref=ref: ref[:, i * HEAD_SIZE : (i + 1) * HEAD_SIZE]
                    for ref in mine
                ],
                [join_lanes(ref[:, part:], repeat) for ref in mine],
                0,
                q_ref,
                k_ref,
                v_ref,
                mask_ref[...],
                o_ref,
                repeat,
            )


def combine_pair(place, near, far, queries, tree_keys, tree_values, mask, repeat):
    rows, width = queries.shape
    part = repeat * HEAD_SIZE
    wide = far[0].shape[2]

    def head(j, p):
        return (0, p[0] % 2 ^ j)

    return pl.pallas_call(
        functools.partial(pair_kernel, repeat=repeat),
        out_shape=jax.ShapeDtypeStruct((1, rows, width), BF16),
        grid_spec=pltpu.PrefetchScalarGridSpec(
            num_scalar_prefetch=1,
            grid=(2,),
            in_specs=[pl.BlockSpec((1, rows, wide), lambda j, p: (0, 0, 0)) for _ in near + far]
            + [
                pl.BlockSpec((rows, part), head),
                pl.BlockSpec((TREE_NODES, HEAD_SIZE), head),
                pl.BlockSpec((TREE_NODES, HEAD_SIZE), head),
                pl.BlockSpec((rows, TREE_NODES), lambda j, p: (0, 0)),
            ],
            out_specs=pl.BlockSpec((1, rows, part), lambda j, p: (0, 0, p[0] % 2 ^ j)),
        ),
        compiler_params=vmem(VMEM_MIB),
        cost_estimate=pl.CostEstimate(
            flops=4 * rows * width * TREE_NODES,
            bytes_accessed=8 * rows * width,
            transcendentals=rows * width // 2,
        ),
        name="combine_pair",
    )(place, *near, *far, queries, tree_keys, tree_values, mask)


def fc_kernel(length_ref, feat_ref, wn_hbm, wp_hbm, o_ref, wn_ref, wp_ref, sems):
    count, block, _ = wn_ref.shape
    copies = []
    for i in range(count):
        rows = pl.ds(i * block, block)
        copies.append(
            (
                pltpu.make_async_copy(wn_hbm.at[rows], wn_ref.at[i], sems.at[0, i]),
                pltpu.make_async_copy(wp_hbm.at[rows], wp_ref.at[i], sems.at[1, i]),
            )
        )
        for copy in copies[-1]:
            copy.start()
    feats = feat_ref[...]
    live, slots = o_ref.shape[0], feats.shape[0]
    shape = (live, slots)
    place, child, step = live_places(length_ref, slots // ACCEPT, shape, 1)
    row = lax.broadcasted_iota(jnp.int32, shape, 0)
    pick = place == row
    prev = (child == row) | ((step == 0) & pick)
    node = dot_nn(pick.astype(F32).astype(BF16), feats).astype(BF16)
    parent = dot_nn(prev.astype(F32).astype(BF16), feats).astype(BF16)
    total = jnp.zeros(o_ref.shape, F32)
    for i in range(count):
        cols = slice(i * block, (i + 1) * block)
        for copy in copies[i]:
            copy.wait()
        total += dot_nn(node[:, cols], wn_ref[i]) + dot_nn(parent[:, cols], wp_ref[i])
    o_ref[...] = total


def fc_project(feats, path_lengths, fc_node, fc_parent):
    slots, width = feats.shape
    live = slots // 2
    cols = fc_node.shape[1]
    block = min(width, 512)
    count = width // block
    return pl.pallas_call(
        fc_kernel,
        out_shape=jax.ShapeDtypeStruct((live, cols), F32),
        in_specs=[
            pl.BlockSpec(memory_space=pltpu.SMEM),
            pl.BlockSpec(memory_space=pltpu.VMEM),
            pl.BlockSpec(memory_space=pl.ANY),
            pl.BlockSpec(memory_space=pl.ANY),
        ],
        scratch_shapes=[
            pltpu.VMEM((count, block, cols), BF16),
            pltpu.VMEM((count, block, cols), BF16),
            pltpu.SemaphoreType.DMA((2, count)),
        ],
        compiler_params=vmem(VMEM_MIB),
        cost_estimate=pl.CostEstimate(
            flops=4 * live * width * cols, bytes_accessed=4 * width * cols, transcendentals=0
        ),
        name="fc_project",
    )(path_lengths, feats, fc_node, fc_parent)


def gate_kernel(xa_ref, xb_ref, gain_ref, wg_ref, wu_ref, o_ref):
    x = xa_ref[...] + xb_ref[...]
    together = o_ref.shape[0]
    units = wg_ref.shape[1] // together
    scaled = (x * gain_ref[...]).astype(BF16)
    squares = jnp.sum(x * x, axis=1, keepdims=True)
    lane = lax.broadcasted_iota(jnp.int32, (x.shape[0], LANES), 1)
    tail = split_lanes(jnp.where(lane == 0, squares, 0.0), 1)
    for t in range(together):
        cols = slice(t * units, (t + 1) * units)
        o_ref[t, :, :units] = dot_nn(scaled, wg_ref[:, cols]).astype(BF16)
        o_ref[t, :, units : 2 * units] = dot_nn(scaled, wu_ref[:, cols]).astype(BF16)
        o_ref[t, :, 2 * units :] = tail


def gate_up(xa, xb, gain, w_gate, w_up, parts):
    live, width = xa.shape
    units = w_gate.shape[1] // parts
    together = 2 if parts % 2 == 0 else 1
    return pl.pallas_call(
        gate_kernel,
        out_shape=jax.ShapeDtypeStruct((parts, live, 2 * units + LANES), BF16),
        grid=(parts // together,),
        in_specs=[
            pl.BlockSpec((live, width), lambda i: (0, 0)),
            pl.BlockSpec((live, width), lambda i: (0, 0)),
            pl.BlockSpec((1, width), lambda i: (0, 0)),
            pl.BlockSpec((width, together * units), lambda i: (0, i)),
            pl.BlockSpec((width, together * units), lambda i: (0, i)),
        ],
        out_specs=pl.BlockSpec((together, live, 2 * units + LANES), lambda i: (i, 0, 0)),
        compiler_params=vmem(VMEM_MIB),
        cost_estimate=pl.CostEstimate(
            flops=4 * live * width * units * parts,
            bytes_accessed=4 * width * units * parts,
            transcendentals=0,
        ),
        name="gate_up",
    )(xa, xb, gain, w_gate, w_up)


def act_kernel(recv_ref, o_ref):
    units = o_ref.shape[2]
    sources = recv_ref.shape[0]
    total = recv_ref[0].astype(F32)
    for c in range(1, sources):
        total += recv_ref[c].astype(F32)
    squares = jnp.sum(total[:, 2 * units :], axis=1, keepdims=True)
    scale = lax.rsqrt(squares / MODEL_WIDTH + 1e-05)
    gate = total[:, :units] * scale
    up = total[:, units : 2 * units] * scale
    hidden = (gate / (1.0 + jnp.exp(-gate)) * up).astype(BF16)
    for c in range(sources):
        o_ref[c] = hidden


def activate(recv):
    sources, live, wide = recv.shape
    units = (wide - LANES) // 2
    return pl.pallas_call(
        act_kernel,
        out_shape=jax.ShapeDtypeStruct((sources, live, units), BF16),
        compiler_params=vmem(VMEM_MIB),
        cost_estimate=pl.CostEstimate(
            flops=recv.size, bytes_accessed=3 * recv.size, transcendentals=live * units
        ),
        name="activate",
    )(recv)


def down_kernel(head_ref, length_ref, hid_ref, xa_ref, xb_ref, w_hbm, o_ref, w_ref, sems):
    parts, units, _ = w_ref.shape
    copies = [
        pltpu.make_async_copy(w_hbm.at[pl.ds(i * units, units)], w_ref.at[i], sems.at[i])
        for i in range(parts)
    ]
    for copy in copies:
        copy.start()
    total = jnp.where(head_ref[0] == 0, xa_ref[...] + xb_ref[...], 0.0)
    slots, live = o_ref.shape[0], total.shape[0]
    place, _, _ = live_places(length_ref, slots // ACCEPT, (slots, live), 0)
    spread = (place == lax.broadcasted_iota(jnp.int32, (slots, live), 1)).astype(F32)
    for i in range(parts):
        copies[i].wait()
        total += dot_nn(hid_ref[i], w_ref[i])
    o_ref[...] = lax.dot_general(
        spread,
        total,
        (((1,), (0,)), ((), ())),
        precision=lax.Precision.HIGHEST,
        preferred_element_type=F32,
    )


def down_project(head, path_lengths, hidden, w_down, xa, xb):
    parts, live, units = hidden.shape
    cols = w_down.shape[1]
    slots = 2 * live
    return pl.pallas_call(
        down_kernel,
        out_shape=jax.ShapeDtypeStruct((slots, cols), F32),
        in_specs=[pl.BlockSpec(memory_space=pltpu.SMEM)] * 2
        + [pl.BlockSpec(memory_space=pltpu.VMEM)] * 3
        + [pl.BlockSpec(memory_space=pl.ANY)],
        scratch_shapes=[
            pltpu.VMEM((parts, units, cols), BF16),
            pltpu.SemaphoreType.DMA((parts,)),
        ],
        compiler_params=vmem(VMEM_MIB),
        cost_estimate=pl.CostEstimate(
            flops=2 * live * parts * units * cols,
            bytes_accessed=2 * parts * units * cols,
            transcendentals=0,
        ),
        name="down_project",
    )(head, path_lengths, hidden, xa, xb, w_down)


def swap(blocks, axis):
    return lax.all_to_all(blocks, axis, split_axis=0, concat_axis=0, tiled=True)


def spread_all(block, axis):
    count = lax.axis_size(axis)
    return swap(jnp.broadcast_to(block[None], (count,) + block.shape), axis)


def partner(value, axis, distance):
    count = lax.axis_size(axis)
    return lax.ppermute(value, axis, [(i, i ^ distance) for i in range(count)])


def shards(
    queries,
    draft_node_keys,
    draft_node_values,
    prompt_keys,
    prompt_values,
    request_group,
    parents,
    node_visibility_mask,
    path_nodes,
    path_lengths,
    fc_node,
    fc_parent,
    norm_gain,
    w_gate,
    w_up,
    w_down,
):
    ctx_count = lax.axis_size("ctx")
    head_count = lax.axis_size("head")
    requests = request_group.shape[0]
    kv_heads = draft_node_keys.shape[1] // HEAD_SIZE
    width = queries.shape[1]
    repeat = width // HEAD_SIZE // kv_heads
    slots = requests * ACCEPT

    paired = kv_heads == 2 and ctx_count % 2 == 0
    me = lax.axis_index("ctx")
    place = me.reshape(1)
    paired = paired and requests == ctx_count == 8
    if paired:
        part = repeat * HEAD_SIZE
        halves = jnp.stack([queries[:, :part], queries[:, part:]])
        outgoing = jnp.broadcast_to(
            halves[None], (ctx_count // 2,) + halves.shape
        ).reshape(ctx_count, TREE_NODES, part)
    else:
        outgoing = None

    mask = node_visibility_mask[0]
    path_spread, path_queries = path_rows(path_nodes, queries, ctx_count)
    path_all = swap(path_spread, "ctx").reshape(slots, width)
    path_part, *traded = path_attend(
        path_all, prompt_keys, prompt_values, request_group, place, kv_heads, repeat, int(paired)
    )
    path_recv = swap(path_part.reshape(requests, ACCEPT, width + LANES), "ctx")
    if paired:
        far_keys, far_values = (partner(block, "ctx", 1) for block in traded)
    features = combine(
        path_nodes,
        path_recv,
        path_queries,
        draft_node_keys,
        draft_node_values,
        mask,
        kv_heads,
        repeat,
        ctx_count,
        "path_combine",
    )
    every_row = swap(features, "ctx").reshape(slots, width)
    if paired:
        every_row, outgoing = lax.optimization_barrier((every_row, outgoing))
        blocks = [prompt_keys, prompt_values, far_keys, far_values]
        bulk_queries = swap(outgoing, "ctx")
    else:
        blocks = [prompt_keys, prompt_values]
        bulk_queries = lax.all_gather(queries, "ctx", axis=0)

    x_total = fc_project(every_row, path_lengths, fc_node, fc_parent)
    distance = 1
    x_other = jnp.zeros_like(x_total)
    while distance < head_count:
        if distance > 1:
            x_total = x_total + x_other
        x_other = partner(x_total, "head", distance)
        distance *= 2

    units = w_gate.shape[1] // ctx_count
    gain = norm_gain[None, :]
    by_lanes = units % LANES == 0
    if by_lanes:
        partial = gate_up(x_total, x_other, gain, w_gate, w_up, ctx_count)
        if paired:
            partial, bulk_queries, *blocks[2:] = lax.optimization_barrier(
                (partial, bulk_queries, *blocks[2:])
            )
        summed = swap(partial, "ctx")
    else:
        x = x_total + x_other
        scaled = (x * gain).astype(BF16)
        both = jnp.stack(
            [
                jnp.dot(scaled, w_gate, preferred_element_type=F32),
                jnp.dot(scaled, w_up, preferred_element_type=F32),
            ]
        )
        both = lax.psum_scatter(both, "ctx", scatter_dimension=2, tiled=True)
        squares = lax.psum(jnp.sum(x * x, axis=1), "ctx")
        summed = both * lax.rsqrt(squares / MODEL_WIDTH + 1e-05)[None, :, None]

    if paired:
        sent = bulk_attend(bulk_queries, blocks, request_group, place, repeat, 1)
        sent, place = lax.optimization_barrier((sent, place))
        kept = bulk_attend(bulk_queries, blocks, request_group, place, repeat, 0)
        near = partner(sent, "ctx", 2)
        summed, kept = lax.optimization_barrier((summed, kept))
    else:
        parts = []
        for k in range(kv_heads):
            cols = slice(k * HEAD_SIZE, (k + 1) * HEAD_SIZE)
            heads = slice(k * repeat * HEAD_SIZE, (k + 1) * repeat * HEAD_SIZE)
            part = bulk_attend(
                bulk_queries[:, :, heads],
                [block[:, :, cols] for block in blocks],
                request_group,
                place,
                repeat,
                None,
            )
            parts.append(
                combine(
                    path_nodes,
                    swap(part, "ctx"),
                    queries[:, heads],
                    draft_node_keys[:, cols],
                    draft_node_values[:, cols],
                    mask,
                    1,
                    repeat,
                    1,
                    "bulk_combine",
                )[0]
            )
        attention_fn = jnp.concatenate(parts, axis=1)

    if by_lanes:
        hidden = activate(summed)
        if paired:
            hidden, near = lax.optimization_barrier((hidden, near))
        hidden_all = swap(hidden, "ctx")
        if paired:
            halves = [kept, near]
            across = partner(fold_blocks(halves, 1, 2, repeat), "ctx", 1)
            further = fold_blocks(halves, 2, 1, repeat)
            mine = fold_blocks(halves, 0, 1, repeat)
            hidden_all, across, further, mine = lax.optimization_barrier(
                (hidden_all, across, further, mine)
            )
            last = [partner(further, "ctx", 4), partner(across[1:], "ctx", 4)]
    else:
        hidden = (jax.nn.silu(summed[0]) * summed[1]).astype(BF16)
        hidden_all = lax.all_gather(hidden, "ctx", axis=1, tiled=True)[None]
    head = lax.axis_index("head").reshape(1)
    expanded = down_project(head, path_lengths, hidden_all, w_down, x_total, x_other)
    if paired:
        expanded, *last = lax.optimization_barrier((expanded, *last))
        attention_fn = combine_pair(
            place, [mine, last[0]], [across, last[1]], queries, draft_node_keys, draft_node_values, mask, repeat
        )[0]
    pieces = swap(expanded.reshape(head_count, slots // head_count, -1), "head")
    draft_out = jnp.sum(pieces, axis=0).astype(BF16)
    return (attention_fn, draft_out)


def solution(mesh):
    return jax.shard_map(
        shards,
        mesh=mesh,
        in_specs=(
            P("ctx", "head"),
            P("ctx", "head"),
            P("ctx", "head"),
            P(None, "ctx", "head"),
            P(None, "ctx", "head"),
            P(),
            P("ctx", None),
            P("ctx", None, None),
            P("ctx", None),
            P(),
            P("head", "ctx"),
            P("head", "ctx"),
            P("ctx"),
            P("ctx", "head"),
            P("ctx", "head"),
            P("head", "ctx"),
        ),
        out_specs=(P("ctx", "head"), P("head", "ctx")),
        check_vma=False,
    )
```

```python
import functools

import jax
import jax.numpy as jnp
from jax import lax
from jax.experimental import pallas as pl
from jax.experimental.pallas import tpu as pltpu
from jax.sharding import PartitionSpec as P

MODEL_WIDTH = 8192
HEAD_SIZE = 128
TREE_NODES = 64
ACCEPT = 8
LANES = 128
LOG2E = 1.4426950408889634
SCORE_BASE2 = HEAD_SIZE ** (-0.5) * LOG2E

VMEM_MIB = 64
BF16 = jnp.bfloat16
F32 = jnp.float32


def dot_nt(a, b):
    return lax.dot_general(a, b, (((1,), (1,)), ((), ())), preferred_element_type=F32)


def dot_nn(a, b):
    return lax.dot_general(a, b, (((1,), (0,)), ((), ())), preferred_element_type=F32)


def split_lanes(stat, width):
    hi = stat.astype(BF16).astype(F32)
    mid = (stat - hi).astype(BF16).astype(F32)
    lo = (stat - hi - mid).astype(BF16).astype(F32)
    packed = hi + pltpu.roll(mid, width, 1) + pltpu.roll(lo, 2 * width, 1)
    return packed.astype(BF16)


def join_lanes(packed, width):
    wide = packed.astype(F32)
    return (
        wide + pltpu.roll(wide, LANES - width, 1) + pltpu.roll(wide, LANES - 2 * width, 1)
    )


def vmem(limit_mib):
    return pltpu.CompilerParams(vmem_limit_bytes=limit_mib << 20)


def one_hot_rows(node_ref, rows):
    row = lax.broadcasted_iota(jnp.int32, (rows, TREE_NODES), 0)
    lane = lax.broadcasted_iota(jnp.int32, (rows, TREE_NODES), 1)
    node = jnp.zeros((rows, TREE_NODES), jnp.int32)
    for i in range(rows):
        node = jnp.where(row == i, node_ref[0, i], node)
    return (lane == node).astype(F32).astype(BF16)


def live_places(length_ref, requests, shape, axis):
    slot = lax.broadcasted_iota(jnp.int32, shape, axis)
    owner, step = slot // ACCEPT, slot % ACCEPT
    place = jnp.full(shape, -1, jnp.int32)
    child = jnp.full(shape, -1, jnp.int32)
    start = jnp.int32(0)
    for r in range(requests):
        length = length_ref[r]
        mine = owner == r
        place = jnp.where(mine & (step < length), start + step, place)
        child = jnp.where(mine & (step + 1 < length), start + step + 1, child)
        start = start + length
    return place, child, step


def query_kernel(node_ref, q_ref, all_ref, own_ref):
    rows = own_ref.shape[0]
    picked = dot_nn(one_hot_rows(node_ref, rows), q_ref[...]).astype(BF16)
    own_ref[...] = picked
    for c in range(all_ref.shape[0]):
        all_ref[c] = picked


def path_rows(path_nodes, queries, copies):
    width = queries.shape[1]
    return pl.pallas_call(
        query_kernel,
        out_shape=[
            jax.ShapeDtypeStruct((copies, ACCEPT, width), BF16),
            jax.ShapeDtypeStruct((ACCEPT, width), BF16),
        ],
        in_specs=[
            pl.BlockSpec(memory_space=pltpu.SMEM),
            pl.BlockSpec(memory_space=pltpu.VMEM),
        ],
        compiler_params=vmem(VMEM_MIB),
        name="path_rows",
    )(path_nodes, queries)


def shard_rows(q_heads, score_fn, mix_fn):
    q = jnp.concatenate(q_heads, axis=0)
    raw = score_fn(q)
    top = jnp.max(raw, axis=1, keepdims=True) * SCORE_BASE2
    weights = jnp.exp2(raw * SCORE_BASE2 - top)
    total = jnp.sum(weights, axis=1, keepdims=True)
    out = (mix_fn(weights) / total).astype(BF16)
    return out, top + jnp.log(total) * LOG2E


def bulk_rows(q_ref, pairs, heads, step, finish):
    nodes = q_ref.shape[1]
    for first in range(0, heads, step):
        q = jnp.concatenate(
            [
                q_ref[0, :, h * HEAD_SIZE : (h + 1) * HEAD_SIZE]
                for h in range(first, first + step)
            ],
            axis=0,
        )
        raws = [dot_nt(q, keys) for keys, _ in pairs]
        tops = [jnp.max(raw, axis=1, keepdims=True) for raw in raws]
        top = functools.reduce(jnp.maximum, tops) * SCORE_BASE2
        total = 0.0
        mixed = 0.0
        for raw, (_, values) in zip(raws, pairs):
            weights = jnp.exp2(raw * SCORE_BASE2 - top)
            total += jnp.sum(weights, axis=1, keepdims=True)
            mixed += dot_nn(weights.astype(BF16), values)
        out = (mixed / total).astype(BF16)
        lse = top + jnp.log(total) * LOG2E
        for i in range(step):
            finish(first + i, out[i * nodes : (i + 1) * nodes], lse[i * nodes : (i + 1) * nodes])


def bulk_kernel(group_ref, place_ref, q_ref, *refs, repeat, which, step):
    blocks, o_ref = refs[:-1], refs[-1]
    nodes = q_ref.shape[1]
    group = group_ref[which(pl.program_id(0), place_ref[0])]
    lane = lax.broadcasted_iota(jnp.int32, (nodes, LANES), 1)
    stat = [jnp.zeros((nodes, LANES), F32)]

    def finish(h, out, lse):
        o_ref[0, :, h * HEAD_SIZE : (h + 1) * HEAD_SIZE] = out
        stat[0] = jnp.where(lane == h, lse, stat[0])

    pairs = [
        (blocks[i][group], blocks[i + 1][group]) for i in range(0, len(blocks), 2)
    ]
    bulk_rows(q_ref, pairs, repeat, step, finish)
    o_ref[0, :, repeat * HEAD_SIZE :] = split_lanes(stat[0], repeat)


def bulk_attend(queries, blocks, groups, place, repeat, odd):
    requests, nodes, width = queries.shape
    turns = requests if odd is None else requests // 2
    out_width = width + LANES
    work = turns * nodes * width * sum(block.shape[1] for block in blocks) // 2

    def which(turn, here):
        if odd is None:
            return turn
        return here ^ (turn // 2 * 4 + odd * 2 + turn % 2)

    def block_map(wide):
        return lambda r, g, c: (0, 0, c[0] % 2 if wide else 0)

    specs = [
        pl.BlockSpec(
            block.shape[:2] + (HEAD_SIZE,),
            block_map(block.shape[2] > HEAD_SIZE),
            pipeline_mode=pl.Buffered(1),
        )
        for block in blocks
    ]
    return pl.pallas_call(
        functools.partial(bulk_kernel, repeat=repeat, which=which, step=min(4, repeat)),
        out_shape=jax.ShapeDtypeStruct((turns, nodes, out_width), BF16),
        grid_spec=pltpu.PrefetchScalarGridSpec(
            num_scalar_prefetch=2,
            grid=(turns,),
            in_specs=[pl.BlockSpec((1, nodes, width), lambda r, g, c: (which(r, c[0]), 0, 0))]
            + specs,
            out_specs=pl.BlockSpec((1, nodes, out_width), lambda r, g, c: (r, 0, 0)),
        ),
        compiler_params=vmem(VMEM_MIB),
        cost_estimate=pl.CostEstimate(
            flops=4 * work, bytes_accessed=8 << 20, transcendentals=work // HEAD_SIZE
        ),
        name="bulk_attend",
    )(groups, place, queries, *blocks)


def path_kernel(group_ref, place_ref, q_ref, k_ref, v_ref, o_ref, *refs, kv_heads, repeat, step, per_block):
    traded, stat_ref = refs[:-1], refs[-1]
    rows_block = q_ref.shape[0]
    heads = kv_heads * repeat
    lane = lax.broadcasted_iota(jnp.int32, (rows_block, LANES), 1)
    owner = lax.broadcasted_iota(jnp.int32, (rows_block, 1), 0) // ACCEPT
    row_group = jnp.zeros((rows_block, 1), jnp.int32)
    for i in range(per_block):
        row_group = jnp.where(
            owner == i, group_ref[pl.program_id(0) * per_block + i], row_group
        )
    first_group = jnp.concatenate([row_group] * step, axis=0) == 0
    k = pl.program_id(1)
    if traded:

        @pl.when(k != place_ref[0] % 2)
        def _():
            traded[0][...] = k_ref[...]
            traded[1][...] = v_ref[...]

    @pl.when(k == 0)
    def _():
        stat_ref[...] = jnp.zeros_like(stat_ref)

    stat = stat_ref[...]
    for first in range(0, repeat, step):
        out, lse = shard_rows(
            [
                q_ref[:, h * HEAD_SIZE : (h + 1) * HEAD_SIZE]
                for h in range(first, first + step)
            ],
            lambda q: jnp.where(first_group, dot_nt(q, k_ref[0]), dot_nt(q, k_ref[1])),
            lambda w: jnp.where(
                first_group,
                dot_nn(w.astype(BF16), v_ref[0]),
                dot_nn(w.astype(BF16), v_ref[1]),
            ),
        )
        for i in range(step):
            h = k * repeat + first + i
            rows = slice(i * rows_block, (i + 1) * rows_block)
            cols = pl.ds(pl.multiple_of(h * HEAD_SIZE, HEAD_SIZE), HEAD_SIZE)
            o_ref[:, cols] = out[rows]
            stat = jnp.where(lane == h, lse[rows], stat)
    stat_ref[...] = stat

    @pl.when(k == kv_heads - 1)
    def _():
        o_ref[:, heads * HEAD_SIZE :] = split_lanes(stat, heads)


def path_attend(rows_all, keys, values, groups, place, kv_heads, repeat, trade):
    rows, width = rows_all.shape
    out_width = width + LANES
    per_block = 8
    block = per_block * ACCEPT
    moved = jax.ShapeDtypeStruct(keys.shape[:2] + (HEAD_SIZE,), BF16)
    work = rows * keys.shape[1] * width
    return pl.pallas_call(
        functools.partial(
            path_kernel,
            kv_heads=kv_heads,
            repeat=repeat,
            step=min(4, repeat),
            per_block=per_block,
        ),
        out_shape=[jax.ShapeDtypeStruct((rows, out_width), BF16)] + [moved] * (2 * trade),
        grid_spec=pltpu.PrefetchScalarGridSpec(
            num_scalar_prefetch=2,
            grid=(rows // block, kv_heads),
            in_specs=[
                pl.BlockSpec((block, width // kv_heads), lambda r, k, g, p: (r, k)),
                pl.BlockSpec(keys.shape[:2] + (HEAD_SIZE,), lambda r, k, g, p: (0, 0, k)),
                pl.BlockSpec(values.shape[:2] + (HEAD_SIZE,), lambda r, k, g, p: (0, 0, k)),
            ],
            out_specs=[pl.BlockSpec((block, out_width), lambda r, k, g, p: (r, 0))]
            + [pl.BlockSpec(moved.shape, lambda r, k, g, p: (0, 0, 0))] * (2 * trade),
            scratch_shapes=[pltpu.VMEM((block, LANES), F32)],
        ),
        compiler_params=vmem(VMEM_MIB),
        cost_estimate=pl.CostEstimate(
            flops=8 * work, bytes_accessed=3 << 20, transcendentals=work // HEAD_SIZE
        ),
        name="path_attend",
    )(groups, place, rows_all, keys, values)


def merge_heads(parts, stats, base, q_ref, k_ref, v_ref, mask, o_ref, repeat):
    rows = q_ref.shape[0]
    copies = o_ref.shape[0]
    best_src = functools.reduce(jnp.maximum, stats)
    q = jnp.concatenate(
        [q_ref[:, i * HEAD_SIZE : (i + 1) * HEAD_SIZE].astype(F32) for i in range(repeat)],
        axis=0,
    ).astype(BF16)
    allowed = jnp.concatenate([mask] * repeat, axis=0) > 0
    raw = jnp.where(allowed, dot_nt(q, k_ref[...]) * SCORE_BASE2, -1e30)
    top = jnp.max(raw, axis=1, keepdims=True)
    weights = jnp.where(allowed, jnp.exp2(raw - top), 0.0)
    total = jnp.sum(weights, axis=1, keepdims=True)
    mixed = dot_nn(weights.astype(BF16), v_ref[...])
    lane = lax.broadcasted_iota(jnp.int32, (rows, LANES), 1)
    for i in range(repeat):
        picked = lane == base + i
        own = slice(i * rows, (i + 1) * rows)

        def column(stat):
            return jnp.sum(jnp.where(picked, stat, 0.0), axis=1, keepdims=True)

        best = jnp.maximum(column(best_src), top[own])
        tree_scale = jnp.exp2(top[own] - best)
        numer = tree_scale * mixed[own]
        denom = tree_scale * total[own]
        for part, stat in zip(parts, stats):
            scale = jnp.exp2(column(stat) - best)
            numer += scale * part(i).astype(F32)
            denom += scale
        out = (numer / denom).astype(BF16)
        for j in range(copies):
            o_ref[j, :, i * HEAD_SIZE : (i + 1) * HEAD_SIZE] = out


def combine_kernel(
    node_ref, recv_ref, stat_ref, q_ref, k_ref, v_ref, mask_ref, o_ref, *, repeat, heads
):
    sources, rows, _ = recv_ref.shape
    mask = mask_ref[...].astype(F32)
    if rows < TREE_NODES:
        mask = dot_nn(one_hot_rows(node_ref, rows), mask.astype(BF16))
    merge_heads(
        [
            lambda i, c=c: recv_ref[c, :, i * HEAD_SIZE : (i + 1) * HEAD_SIZE]
            for c in range(sources)
        ],
        [join_lanes(stat_ref[c], heads) for c in range(sources)],
        pl.program_id(0) * repeat,
        q_ref,
        k_ref,
        v_ref,
        mask,
        o_ref,
        repeat,
    )


def combine(path_nodes, recv, queries, tree_keys, tree_values, mask, kv_heads, repeat, copies, name):
    sources, rows, wide = recv.shape
    width = wide - LANES
    part = repeat * HEAD_SIZE
    return pl.pallas_call(
        functools.partial(combine_kernel, repeat=repeat, heads=kv_heads * repeat),
        out_shape=jax.ShapeDtypeStruct((copies, rows, width), BF16),
        grid=(kv_heads,),
        in_specs=[
            pl.BlockSpec(memory_space=pltpu.SMEM),
            pl.BlockSpec((sources, rows, part), lambda k: (0, 0, k)),
            pl.BlockSpec((sources, rows, LANES), lambda k: (0, 0, width // LANES)),
            pl.BlockSpec((rows, part), lambda k: (0, k)),
            pl.BlockSpec((TREE_NODES, HEAD_SIZE), lambda k: (0, k)),
            pl.BlockSpec((TREE_NODES, HEAD_SIZE), lambda k: (0, k)),
            pl.BlockSpec((TREE_NODES, TREE_NODES), lambda k: (0, 0)),
        ],
        out_specs=pl.BlockSpec((copies, rows, part), lambda k: (0, 0, k)),
        compiler_params=vmem(VMEM_MIB),
        cost_estimate=pl.CostEstimate(
            flops=4 * rows * width * TREE_NODES,
            bytes_accessed=2 * recv.size + 4 * rows * width,
            transcendentals=rows * width // 2,
        ),
        name=name,
    )(path_nodes, recv, recv, queries, tree_keys, tree_values, mask)


def fold_kernel(*refs, repeat):
    sources, o_ref = refs[:-1], refs[-1]
    rows = o_ref.shape[1]
    part = repeat * HEAD_SIZE
    lane = lax.broadcasted_iota(jnp.int32, (rows, LANES), 1)
    stats = [join_lanes(ref[0, :, part:], repeat) for ref in sources]
    best = functools.reduce(jnp.maximum, stats)
    scales = [jnp.exp2(stat - best) for stat in stats]
    total = functools.reduce(jnp.add, scales)
    for i in range(repeat):
        cols = slice(i * HEAD_SIZE, (i + 1) * HEAD_SIZE)

        def column(stat):
            return jnp.sum(jnp.where(lane == i, stat, 0.0), axis=1, keepdims=True)

        numer = 0.0
        for ref, scale in zip(sources, scales):
            numer += column(scale) * ref[0, :, cols].astype(F32)
        o_ref[0, :, cols] = (numer / column(total)).astype(BF16)
    lse = best + jnp.log(total) * LOG2E
    o_ref[0, :, part:] = split_lanes(jnp.where(lane < repeat, lse, 0.0), repeat)


def fold_blocks(sources, first, count, repeat):
    _, rows, wide = sources[0].shape
    return pl.pallas_call(
        functools.partial(fold_kernel, repeat=repeat),
        out_shape=jax.ShapeDtypeStruct((count, rows, wide), BF16),
        grid=(count,),
        in_specs=[
            pl.BlockSpec((1, rows, wide), lambda j: (first + 2 * j, 0, 0)) for _ in sources
        ],
        out_specs=pl.BlockSpec((1, rows, wide), lambda j: (j, 0, 0)),
        compiler_params=vmem(VMEM_MIB),
        cost_estimate=pl.CostEstimate(
            flops=rows * wide, bytes_accessed=6 * rows * wide, transcendentals=0
        ),
        name="fold_blocks",
    )(*sources)


def pair_kernel(place_ref, *refs, repeat):
    count = (len(refs) - 5) // 2
    near, far, rest = refs[:count], refs[count:-5], refs[-5:]
    q_ref, k_ref, v_ref, mask_ref, o_ref = rest
    part = repeat * HEAD_SIZE
    for turn in range(2):

        @pl.when(pl.program_id(0) == turn)
        def _(turn=turn):
            mine = [ref.at[0] for ref in (near if turn == 0 else far)]
            merge_heads(
                [
                    lambda i, ref=ref: ref[:, i * HEAD_SIZE : (i + 1) * HEAD_SIZE]
                    for ref in mine
                ],
                [join_lanes(ref[:, part:], repeat) for ref in mine],
                0,
                q_ref,
                k_ref,
                v_ref,
                mask_ref[...],
                o_ref,
                repeat,
            )


def combine_pair(place, near, far, queries, tree_keys, tree_values, mask, repeat):
    rows, width = queries.shape
    part = repeat * HEAD_SIZE
    wide = far[0].shape[2]

    def head(j, p):
        return (0, p[0] % 2 ^ j)

    return pl.pallas_call(
        functools.partial(pair_kernel, repeat=repeat),
        out_shape=jax.ShapeDtypeStruct((1, rows, width), BF16),
        grid_spec=pltpu.PrefetchScalarGridSpec(
            num_scalar_prefetch=1,
            grid=(2,),
            in_specs=[pl.BlockSpec((1, rows, wide), lambda j, p: (0, 0, 0)) for _ in near + far]
            + [
                pl.BlockSpec((rows, part), head),
                pl.BlockSpec((TREE_NODES, HEAD_SIZE), head),
                pl.BlockSpec((TREE_NODES, HEAD_SIZE), head),
                pl.BlockSpec((rows, TREE_NODES), lambda j, p: (0, 0)),
            ],
            out_specs=pl.BlockSpec((1, rows, part), lambda j, p: (0, 0, p[0] % 2 ^ j)),
        ),
        compiler_params=vmem(VMEM_MIB),
        cost_estimate=pl.CostEstimate(
            flops=4 * rows * width * TREE_NODES,
            bytes_accessed=8 * rows * width,
            transcendentals=rows * width // 2,
        ),
        name="combine_pair",
    )(place, *near, *far, queries, tree_keys, tree_values, mask)


def fc_kernel(length_ref, feat_ref, wn_hbm, wp_hbm, o_ref, wn_ref, wp_ref, sems):
    count, block, _ = wn_ref.shape
    copies = []
    for i in range(count):
        rows = pl.ds(i * block, block)
        copies.append(
            (
                pltpu.make_async_copy(wn_hbm.at[rows], wn_ref.at[i], sems.at[0, i]),
                pltpu.make_async_copy(wp_hbm.at[rows], wp_ref.at[i], sems.at[1, i]),
            )
        )
        for copy in copies[-1]:
            copy.start()
    feats = feat_ref[...]
    live, slots = o_ref.shape[0], feats.shape[0]
    shape = (live, slots)
    place, child, step = live_places(length_ref, slots // ACCEPT, shape, 1)
    row = lax.broadcasted_iota(jnp.int32, shape, 0)
    pick = place == row
    prev = (child == row) | ((step == 0) & pick)
    node = dot_nn(pick.astype(F32).astype(BF16), feats).astype(BF16)
    parent = dot_nn(prev.astype(F32).astype(BF16), feats).astype(BF16)
    total = jnp.zeros(o_ref.shape, F32)
    for i in range(count):
        cols = slice(i * block, (i + 1) * block)
        for copy in copies[i]:
            copy.wait()
        total += dot_nn(node[:, cols], wn_ref[i]) + dot_nn(parent[:, cols], wp_ref[i])
    o_ref[...] = total


def fc_project(feats, path_lengths, fc_node, fc_parent):
    slots, width = feats.shape
    live = slots // 2
    cols = fc_node.shape[1]
    block = min(width, 512)
    count = width // block
    return pl.pallas_call(
        fc_kernel,
        out_shape=jax.ShapeDtypeStruct((live, cols), F32),
        in_specs=[
            pl.BlockSpec(memory_space=pltpu.SMEM),
            pl.BlockSpec(memory_space=pltpu.VMEM),
            pl.BlockSpec(memory_space=pl.ANY),
            pl.BlockSpec(memory_space=pl.ANY),
        ],
        scratch_shapes=[
            pltpu.VMEM((count, block, cols), BF16),
            pltpu.VMEM((count, block, cols), BF16),
            pltpu.SemaphoreType.DMA((2, count)),
        ],
        compiler_params=vmem(VMEM_MIB),
        cost_estimate=pl.CostEstimate(
            flops=4 * live * width * cols, bytes_accessed=4 * width * cols, transcendentals=0
        ),
        name="fc_project",
    )(path_lengths, feats, fc_node, fc_parent)


def gate_kernel(xa_ref, xb_ref, gain_ref, wg_ref, wu_ref, o_ref):
    x = xa_ref[...] + xb_ref[...]
    together = o_ref.shape[0]
    units = wg_ref.shape[1] // together
    scaled = (x * gain_ref[...]).astype(BF16)
    squares = jnp.sum(x * x, axis=1, keepdims=True)
    lane = lax.broadcasted_iota(jnp.int32, (x.shape[0], LANES), 1)
    tail = split_lanes(jnp.where(lane == 0, squares, 0.0), 1)
    for t in range(together):
        cols = slice(t * units, (t + 1) * units)
        o_ref[t, :, :units] = dot_nn(scaled, wg_ref[:, cols]).astype(BF16)
        o_ref[t, :, units : 2 * units] = dot_nn(scaled, wu_ref[:, cols]).astype(BF16)
        o_ref[t, :, 2 * units :] = tail


def gate_up(xa, xb, gain, w_gate, w_up, parts):
    live, width = xa.shape
    units = w_gate.shape[1] // parts
    together = 2 if parts % 2 == 0 else 1
    return pl.pallas_call(
        gate_kernel,
        out_shape=jax.ShapeDtypeStruct((parts, live, 2 * units + LANES), BF16),
        grid=(parts // together,),
        in_specs=[
            pl.BlockSpec((live, width), lambda i: (0, 0)),
            pl.BlockSpec((live, width), lambda i: (0, 0)),
            pl.BlockSpec((1, width), lambda i: (0, 0)),
            pl.BlockSpec((width, together * units), lambda i: (0, i)),
            pl.BlockSpec((width, together * units), lambda i: (0, i)),
        ],
        out_specs=pl.BlockSpec((together, live, 2 * units + LANES), lambda i: (i, 0, 0)),
        compiler_params=vmem(VMEM_MIB),
        cost_estimate=pl.CostEstimate(
            flops=4 * live * width * units * parts,
            bytes_accessed=4 * width * units * parts,
            transcendentals=0,
        ),
        name="gate_up",
    )(xa, xb, gain, w_gate, w_up)


def act_kernel(recv_ref, o_ref):
    units = o_ref.shape[2]
    sources = recv_ref.shape[0]
    total = recv_ref[0].astype(F32)
    for c in range(1, sources):
        total += recv_ref[c].astype(F32)
    squares = jnp.sum(total[:, 2 * units :], axis=1, keepdims=True)
    scale = lax.rsqrt(squares / MODEL_WIDTH + 1e-05)
    gate = total[:, :units] * scale
    up = total[:, units : 2 * units] * scale
    hidden = (gate / (1.0 + jnp.exp(-gate)) * up).astype(BF16)
    for c in range(sources):
        o_ref[c] = hidden


def activate(recv):
    sources, live, wide = recv.shape
    units = (wide - LANES) // 2
    return pl.pallas_call(
        act_kernel,
        out_shape=jax.ShapeDtypeStruct((sources, live, units), BF16),
        compiler_params=vmem(VMEM_MIB),
        cost_estimate=pl.CostEstimate(
            flops=recv.size, bytes_accessed=3 * recv.size, transcendentals=live * units
        ),
        name="activate",
    )(recv)


def down_kernel(head_ref, length_ref, hid_ref, xa_ref, xb_ref, w_hbm, o_ref, w_ref, sems):
    parts, units, _ = w_ref.shape
    copies = [
        pltpu.make_async_copy(w_hbm.at[pl.ds(i * units, units)], w_ref.at[i], sems.at[i])
        for i in range(parts)
    ]
    for copy in copies:
        copy.start()
    total = jnp.where(head_ref[0] == 0, xa_ref[...] + xb_ref[...], 0.0)
    slots, live = o_ref.shape[0], total.shape[0]
    place, _, _ = live_places(length_ref, slots // ACCEPT, (slots, live), 0)
    spread = (place == lax.broadcasted_iota(jnp.int32, (slots, live), 1)).astype(F32)
    for i in range(parts):
        copies[i].wait()
        total += dot_nn(hid_ref[i], w_ref[i])
    o_ref[...] = lax.dot_general(
        spread,
        total,
        (((1,), (0,)), ((), ())),
        precision=lax.Precision.HIGHEST,
        preferred_element_type=F32,
    )


def down_project(head, path_lengths, hidden, w_down, xa, xb):
    parts, live, units = hidden.shape
    cols = w_down.shape[1]
    slots = 2 * live
    return pl.pallas_call(
        down_kernel,
        out_shape=jax.ShapeDtypeStruct((slots, cols), F32),
        in_specs=[pl.BlockSpec(memory_space=pltpu.SMEM)] * 2
        + [pl.BlockSpec(memory_space=pltpu.VMEM)] * 3
        + [pl.BlockSpec(memory_space=pl.ANY)],
        scratch_shapes=[
            pltpu.VMEM((parts, units, cols), BF16),
            pltpu.SemaphoreType.DMA((parts,)),
        ],
        compiler_params=vmem(VMEM_MIB),
        cost_estimate=pl.CostEstimate(
            flops=2 * live * parts * units * cols,
            bytes_accessed=2 * parts * units * cols,
            transcendentals=0,
        ),
        name="down_project",
    )(head, path_lengths, hidden, xa, xb, w_down)


def swap(blocks, axis):
    return lax.all_to_all(blocks, axis, split_axis=0, concat_axis=0, tiled=True)


def spread_all(block, axis):
    count = lax.axis_size(axis)
    return swap(jnp.broadcast_to(block[None], (count,) + block.shape), axis)


def partner(value, axis, distance):
    count = lax.axis_size(axis)
    return lax.ppermute(value, axis, [(i, i ^ distance) for i in range(count)])


def shards(
    queries,
    draft_node_keys,
    draft_node_values,
    prompt_keys,
    prompt_values,
    request_group,
    parents,
    node_visibility_mask,
    path_nodes,
    path_lengths,
    fc_node,
    fc_parent,
    norm_gain,
    w_gate,
    w_up,
    w_down,
):
    ctx_count = lax.axis_size("ctx")
    head_count = lax.axis_size("head")
    requests = request_group.shape[0]
    kv_heads = draft_node_keys.shape[1] // HEAD_SIZE
    width = queries.shape[1]
    repeat = width // HEAD_SIZE // kv_heads
    slots = requests * ACCEPT

    paired = kv_heads == 2 and ctx_count % 2 == 0
    me = lax.axis_index("ctx")
    place = me.reshape(1)
    paired = paired and requests == ctx_count == 8
    if paired:
        part = repeat * HEAD_SIZE
        halves = jnp.stack([queries[:, :part], queries[:, part:]])
        outgoing = jnp.broadcast_to(
            halves[None], (ctx_count // 2,) + halves.shape
        ).reshape(ctx_count, TREE_NODES, part)
    else:
        outgoing = None

    mask = node_visibility_mask[0]
    path_spread, path_queries = path_rows(path_nodes, queries, ctx_count)
    path_all = swap(path_spread, "ctx").reshape(slots, width)
    path_part, *traded = path_attend(
        path_all, prompt_keys, prompt_values, request_group, place, kv_heads, repeat, int(paired)
    )
    path_recv = swap(path_part.reshape(requests, ACCEPT, width + LANES), "ctx")
    if paired:
        far_keys, far_values = (partner(block, "ctx", 1) for block in traded)
    features = combine(
        path_nodes,
        path_recv,
        path_queries,
        draft_node_keys,
        draft_node_values,
        mask,
        kv_heads,
        repeat,
        ctx_count,
        "path_combine",
    )
    every_row = swap(features, "ctx").reshape(slots, width)
    if paired:
        every_row, outgoing, far_keys = lax.optimization_barrier((every_row, outgoing, far_keys))
        blocks = [prompt_keys, prompt_values, far_keys, far_values]
        bulk_queries = swap(outgoing, "ctx")
    else:
        blocks = [prompt_keys, prompt_values]
        bulk_queries = lax.all_gather(queries, "ctx", axis=0)

    x_total = fc_project(every_row, path_lengths, fc_node, fc_parent)
    distance = 1
    x_other = jnp.zeros_like(x_total)
    while distance < head_count:
        if distance > 1:
            x_total = x_total + x_other
        x_other = partner(x_total, "head", distance)
        distance *= 2

    units = w_gate.shape[1] // ctx_count
    gain = norm_gain[None, :]
    by_lanes = units % LANES == 0
    if by_lanes:
        partial = gate_up(x_total, x_other, gain, w_gate, w_up, ctx_count)
        if paired:
            partial, bulk_queries, *blocks[2:] = lax.optimization_barrier(
                (partial, bulk_queries, *blocks[2:])
            )
        summed = swap(partial, "ctx")
    else:
        x = x_total + x_other
        scaled = (x * gain).astype(BF16)
        both = jnp.stack(
            [
                jnp.dot(scaled, w_gate, preferred_element_type=F32),
                jnp.dot(scaled, w_up, preferred_element_type=F32),
            ]
        )
        both = lax.psum_scatter(both, "ctx", scatter_dimension=2, tiled=True)
        squares = lax.psum(jnp.sum(x * x, axis=1), "ctx")
        summed = both * lax.rsqrt(squares / MODEL_WIDTH + 1e-05)[None, :, None]

    if paired:
        sent = bulk_attend(bulk_queries, blocks, request_group, place, repeat, 1)
        sent, place = lax.optimization_barrier((sent, place))
        kept = bulk_attend(bulk_queries, blocks, request_group, place, repeat, 0)
        near = partner(sent, "ctx", 2)
        summed, kept = lax.optimization_barrier((summed, kept))
    else:
        parts = []
        for k in range(kv_heads):
            cols = slice(k * HEAD_SIZE, (k + 1) * HEAD_SIZE)
            heads = slice(k * repeat * HEAD_SIZE, (k + 1) * repeat * HEAD_SIZE)
            part = bulk_attend(
                bulk_queries[:, :, heads],
                [block[:, :, cols] for block in blocks],
                request_group,
                place,
                repeat,
                None,
            )
            parts.append(
                combine(
                    path_nodes,
                    swap(part, "ctx"),
                    queries[:, heads],
                    draft_node_keys[:, cols],
                    draft_node_values[:, cols],
                    mask,
                    1,
                    repeat,
                    1,
                    "bulk_combine",
                )[0]
            )
        attention_fn = jnp.concatenate(parts, axis=1)

    if by_lanes:
        hidden = activate(summed)
        if paired:
            hidden, near = lax.optimization_barrier((hidden, near))
        hidden_all = swap(hidden, "ctx")
        if paired:
            halves = [kept, near]
            across = [partner(fold_blocks(halves, n, 1, repeat), "ctx", 1) for n in (3, 1)]
            further = fold_blocks(halves, 2, 1, repeat)
            mine = fold_blocks(halves, 0, 1, repeat)
            hidden_all, across[0], further, mine = lax.optimization_barrier(
                (hidden_all, across[0], further, mine)
            )
            last = [partner(block, "ctx", 4) for block in (further, across[0])]
    else:
        hidden = (jax.nn.silu(summed[0]) * summed[1]).astype(BF16)
        hidden_all = lax.all_gather(hidden, "ctx", axis=1, tiled=True)[None]
    head = lax.axis_index("head").reshape(1)
    expanded = down_project(head, path_lengths, hidden_all, w_down, x_total, x_other)
    if paired:
        expanded, across[1], *last = lax.optimization_barrier((expanded, across[1], *last))
        attention_fn = combine_pair(
            place, [mine, last[0]], [across[1], last[1]], queries, draft_node_keys, draft_node_values, mask, repeat
        )[0]
    pieces = swap(expanded.reshape(head_count, slots // head_count, -1), "head")
    draft_out = jnp.sum(pieces, axis=0).astype(BF16)
    return (attention_fn, draft_out)


def solution(mesh):
    return jax.shard_map(
        shards,
        mesh=mesh,
        in_specs=(
            P("ctx", "head"),
            P("ctx", "head"),
            P("ctx", "head"),
            P(None, "ctx", "head"),
            P(None, "ctx", "head"),
            P(),
            P("ctx", None),
            P("ctx", None, None),
            P("ctx", None),
            P(),
            P("head", "ctx"),
            P("head", "ctx"),
            P("ctx"),
            P("ctx", "head"),
            P("ctx", "head"),
            P("head", "ctx"),
        ),
        out_specs=(P("ctx", "head"), P("head", "ctx")),
        check_vma=False,
    )
```

```python
import functools

import jax
import jax.numpy as jnp
from jax import lax
from jax.experimental import pallas as pl
from jax.experimental.pallas import tpu as pltpu
from jax.sharding import PartitionSpec as P

MODEL_WIDTH = 8192
HEAD_SIZE = 128
TREE_NODES = 64
ACCEPT = 8
LANES = 128
LOG2E = 1.4426950408889634
SCORE_BASE2 = HEAD_SIZE ** (-0.5) * LOG2E

VMEM_MIB = 64
BF16 = jnp.bfloat16
F32 = jnp.float32


def dot_nt(a, b):
    return lax.dot_general(a, b, (((1,), (1,)), ((), ())), preferred_element_type=F32)


def dot_nn(a, b):
    return lax.dot_general(a, b, (((1,), (0,)), ((), ())), preferred_element_type=F32)


def split_lanes(stat, width):
    hi = stat.astype(BF16).astype(F32)
    mid = (stat - hi).astype(BF16).astype(F32)
    lo = (stat - hi - mid).astype(BF16).astype(F32)
    packed = hi + pltpu.roll(mid, width, 1) + pltpu.roll(lo, 2 * width, 1)
    return packed.astype(BF16)


def join_lanes(packed, width):
    wide = packed.astype(F32)
    return (
        wide + pltpu.roll(wide, LANES - width, 1) + pltpu.roll(wide, LANES - 2 * width, 1)
    )


def vmem(limit_mib):
    return pltpu.CompilerParams(vmem_limit_bytes=limit_mib << 20)


def one_hot_rows(node_ref, rows):
    row = lax.broadcasted_iota(jnp.int32, (rows, TREE_NODES), 0)
    lane = lax.broadcasted_iota(jnp.int32, (rows, TREE_NODES), 1)
    node = jnp.zeros((rows, TREE_NODES), jnp.int32)
    for i in range(rows):
        node = jnp.where(row == i, node_ref[0, i], node)
    return (lane == node).astype(F32).astype(BF16)


def live_places(length_ref, requests, shape, axis, base=0):
    slot = lax.broadcasted_iota(jnp.int32, shape, axis) + base
    owner, step = slot // ACCEPT, slot % ACCEPT
    place = jnp.full(shape, -1, jnp.int32)
    child = jnp.full(shape, -1, jnp.int32)
    start = jnp.int32(0)
    for r in range(requests):
        length = length_ref[r]
        mine = owner == r
        place = jnp.where(mine & (step < length), start + step, place)
        child = jnp.where(mine & (step + 1 < length), start + step + 1, child)
        start = start + length
    return place, child, step


def query_kernel(node_ref, q_ref, all_ref, own_ref):
    rows = own_ref.shape[0]
    picked = dot_nn(one_hot_rows(node_ref, rows), q_ref[...]).astype(BF16)
    own_ref[...] = picked
    for c in range(all_ref.shape[0]):
        all_ref[c] = picked


def path_rows(path_nodes, queries, copies):
    width = queries.shape[1]
    return pl.pallas_call(
        query_kernel,
        out_shape=[
            jax.ShapeDtypeStruct((copies, ACCEPT, width), BF16),
            jax.ShapeDtypeStruct((ACCEPT, width), BF16),
        ],
        in_specs=[
            pl.BlockSpec(memory_space=pltpu.SMEM),
            pl.BlockSpec(memory_space=pltpu.VMEM),
        ],
        compiler_params=vmem(VMEM_MIB),
        name="path_rows",
    )(path_nodes, queries)


def shard_rows(q_heads, score_fn, mix_fn):
    q = jnp.concatenate(q_heads, axis=0)
    raw = score_fn(q)
    top = jnp.max(raw, axis=1, keepdims=True) * SCORE_BASE2
    weights = jnp.exp2(raw * SCORE_BASE2 - top)
    total = jnp.sum(weights, axis=1, keepdims=True)
    out = (mix_fn(weights) / total).astype(BF16)
    return out, top + jnp.log(total) * LOG2E


def bulk_rows(q_ref, pairs, heads, step, finish):
    nodes = q_ref.shape[1]
    for first in range(0, heads, step):
        q = jnp.concatenate(
            [
                q_ref[0, :, h * HEAD_SIZE : (h + 1) * HEAD_SIZE]
                for h in range(first, first + step)
            ],
            axis=0,
        )
        raws = [dot_nt(q, keys) for keys, _ in pairs]
        tops = [jnp.max(raw, axis=1, keepdims=True) for raw in raws]
        top = functools.reduce(jnp.maximum, tops) * SCORE_BASE2
        total = 0.0
        mixed = 0.0
        for raw, (_, values) in zip(raws, pairs):
            weights = jnp.exp2(raw * SCORE_BASE2 - top)
            total += jnp.sum(weights, axis=1, keepdims=True)
            mixed += dot_nn(weights.astype(BF16), values)
        out = (mixed / total).astype(BF16)
        lse = top + jnp.log(total) * LOG2E
        for i in range(step):
            finish(first + i, out[i * nodes : (i + 1) * nodes], lse[i * nodes : (i + 1) * nodes])


def bulk_kernel(group_ref, place_ref, q_ref, *refs, repeat, which, step):
    blocks, o_ref = refs[:-1], refs[-1]
    nodes = q_ref.shape[1]
    group = group_ref[which(pl.program_id(0), place_ref[0])]
    lane = lax.broadcasted_iota(jnp.int32, (nodes, LANES), 1)
    stat = [jnp.zeros((nodes, LANES), F32)]

    def finish(h, out, lse):
        o_ref[0, :, h * HEAD_SIZE : (h + 1) * HEAD_SIZE] = out
        stat[0] = jnp.where(lane == h, lse, stat[0])

    pairs = [
        (blocks[i][group], blocks[i + 1][group]) for i in range(0, len(blocks), 2)
    ]
    bulk_rows(q_ref, pairs, repeat, step, finish)
    o_ref[0, :, repeat * HEAD_SIZE :] = split_lanes(stat[0], repeat)


def bulk_attend(queries, blocks, groups, place, repeat, odd):
    requests, nodes, width = queries.shape
    turns = requests if odd is None else requests // 2
    out_width = width + LANES
    work = turns * nodes * width * sum(block.shape[1] for block in blocks) // 2

    def which(turn, here):
        if odd is None:
            return turn
        return here ^ (turn // 2 * 4 + odd * 2 + turn % 2)

    def block_map(wide):
        return lambda r, g, c: (0, 0, c[0] % 2 if wide else 0)

    specs = [
        pl.BlockSpec(
            block.shape[:2] + (HEAD_SIZE,),
            block_map(block.shape[2] > HEAD_SIZE),
            pipeline_mode=pl.Buffered(1),
        )
        for block in blocks
    ]
    return pl.pallas_call(
        functools.partial(bulk_kernel, repeat=repeat, which=which, step=min(4, repeat)),
        out_shape=jax.ShapeDtypeStruct((turns, nodes, out_width), BF16),
        grid_spec=pltpu.PrefetchScalarGridSpec(
            num_scalar_prefetch=2,
            grid=(turns,),
            in_specs=[pl.BlockSpec((1, nodes, width), lambda r, g, c: (which(r, c[0]), 0, 0))]
            + specs,
            out_specs=pl.BlockSpec((1, nodes, out_width), lambda r, g, c: (r, 0, 0)),
        ),
        compiler_params=vmem(VMEM_MIB),
        cost_estimate=pl.CostEstimate(
            flops=4 * work, bytes_accessed=8 << 20, transcendentals=work // HEAD_SIZE
        ),
        name="bulk_attend",
    )(groups, place, queries, *blocks)


def path_kernel(group_ref, place_ref, q_ref, k_ref, v_ref, o_ref, *refs, kv_heads, repeat, step, per_block):
    traded, stat_ref = refs[:-1], refs[-1]
    rows_block = q_ref.shape[0]
    heads = kv_heads * repeat
    lane = lax.broadcasted_iota(jnp.int32, (rows_block, LANES), 1)
    owner = lax.broadcasted_iota(jnp.int32, (rows_block, 1), 0) // ACCEPT
    row_group = jnp.zeros((rows_block, 1), jnp.int32)
    for i in range(per_block):
        row_group = jnp.where(
            owner == i, group_ref[pl.program_id(0) * per_block + i], row_group
        )
    first_group = jnp.concatenate([row_group] * step, axis=0) == 0
    k = pl.program_id(1)
    if traded:

        @pl.when(k != place_ref[0] % 2)
        def _():
            traded[0][...] = k_ref[...]
            traded[1][...] = v_ref[...]

    @pl.when(k == 0)
    def _():
        stat_ref[...] = jnp.zeros_like(stat_ref)

    stat = stat_ref[...]
    for first in range(0, repeat, step):
        out, lse = shard_rows(
            [
                q_ref[:, h * HEAD_SIZE : (h + 1) * HEAD_SIZE]
                for h in range(first, first + step)
            ],
            lambda q: jnp.where(first_group, dot_nt(q, k_ref[0]), dot_nt(q, k_ref[1])),
            lambda w: jnp.where(
                first_group,
                dot_nn(w.astype(BF16), v_ref[0]),
                dot_nn(w.astype(BF16), v_ref[1]),
            ),
        )
        for i in range(step):
            h = k * repeat + first + i
            rows = slice(i * rows_block, (i + 1) * rows_block)
            cols = pl.ds(pl.multiple_of(h * HEAD_SIZE, HEAD_SIZE), HEAD_SIZE)
            o_ref[:, cols] = out[rows]
            stat = jnp.where(lane == h, lse[rows], stat)
    stat_ref[...] = stat

    @pl.when(k == kv_heads - 1)
    def _():
        o_ref[:, heads * HEAD_SIZE :] = split_lanes(stat, heads)


def path_attend(rows_all, keys, values, groups, place, kv_heads, repeat, trade):
    rows, width = rows_all.shape
    out_width = width + LANES
    per_block = 8
    block = per_block * ACCEPT
    moved = jax.ShapeDtypeStruct(keys.shape[:2] + (HEAD_SIZE,), BF16)
    work = rows * keys.shape[1] * width
    return pl.pallas_call(
        functools.partial(
            path_kernel,
            kv_heads=kv_heads,
            repeat=repeat,
            step=min(4, repeat),
            per_block=per_block,
        ),
        out_shape=[jax.ShapeDtypeStruct((rows, out_width), BF16)] + [moved] * (2 * trade),
        grid_spec=pltpu.PrefetchScalarGridSpec(
            num_scalar_prefetch=2,
            grid=(rows // block, kv_heads),
            in_specs=[
                pl.BlockSpec((block, width // kv_heads), lambda r, k, g, p: (r, k)),
                pl.BlockSpec(keys.shape[:2] + (HEAD_SIZE,), lambda r, k, g, p: (0, 0, k)),
                pl.BlockSpec(values.shape[:2] + (HEAD_SIZE,), lambda r, k, g, p: (0, 0, k)),
            ],
            out_specs=[pl.BlockSpec((block, out_width), lambda r, k, g, p: (r, 0))]
            + [pl.BlockSpec(moved.shape, lambda r, k, g, p: (0, 0, 0))] * (2 * trade),
            scratch_shapes=[pltpu.VMEM((block, LANES), F32)],
        ),
        compiler_params=vmem(VMEM_MIB),
        cost_estimate=pl.CostEstimate(
            flops=8 * work, bytes_accessed=3 << 20, transcendentals=work // HEAD_SIZE
        ),
        name="path_attend",
    )(groups, place, rows_all, keys, values)


def merge_heads(parts, stats, base, q_ref, k_ref, v_ref, mask, o_ref, repeat):
    rows = q_ref.shape[0]
    copies = o_ref.shape[0]
    best_src = functools.reduce(jnp.maximum, stats)
    q = jnp.concatenate(
        [q_ref[:, i * HEAD_SIZE : (i + 1) * HEAD_SIZE].astype(F32) for i in range(repeat)],
        axis=0,
    ).astype(BF16)
    allowed = jnp.concatenate([mask] * repeat, axis=0) > 0
    raw = jnp.where(allowed, dot_nt(q, k_ref[...]) * SCORE_BASE2, -1e30)
    top = jnp.max(raw, axis=1, keepdims=True)
    weights = jnp.where(allowed, jnp.exp2(raw - top), 0.0)
    total = jnp.sum(weights, axis=1, keepdims=True)
    mixed = dot_nn(weights.astype(BF16), v_ref[...])
    lane = lax.broadcasted_iota(jnp.int32, (rows, LANES), 1)
    for i in range(repeat):
        picked = lane == base + i
        own = slice(i * rows, (i + 1) * rows)

        def column(stat):
            return jnp.sum(jnp.where(picked, stat, 0.0), axis=1, keepdims=True)

        best = jnp.maximum(column(best_src), top[own])
        tree_scale = jnp.exp2(top[own] - best)
        numer = tree_scale * mixed[own]
        denom = tree_scale * total[own]
        for part, stat in zip(parts, stats):
            scale = jnp.exp2(column(stat) - best)
            numer += scale * part(i).astype(F32)
            denom += scale
        out = (numer / denom).astype(BF16)
        for j in range(copies):
            o_ref[j, :, i * HEAD_SIZE : (i + 1) * HEAD_SIZE] = out


def combine_kernel(
    node_ref, recv_ref, stat_ref, q_ref, k_ref, v_ref, mask_ref, o_ref, *, repeat, heads
):
    sources, rows, _ = recv_ref.shape
    mask = mask_ref[...].astype(F32)
    if rows < TREE_NODES:
        mask = dot_nn(one_hot_rows(node_ref, rows), mask.astype(BF16))
    merge_heads(
        [
            lambda i, c=c: recv_ref[c, :, i * HEAD_SIZE : (i + 1) * HEAD_SIZE]
            for c in range(sources)
        ],
        [join_lanes(stat_ref[c], heads) for c in range(sources)],
        pl.program_id(0) * repeat,
        q_ref,
        k_ref,
        v_ref,
        mask,
        o_ref,
        repeat,
    )


def combine(path_nodes, recv, queries, tree_keys, tree_values, mask, kv_heads, repeat, copies, name):
    sources, rows, wide = recv.shape
    width = wide - LANES
    part = repeat * HEAD_SIZE
    return pl.pallas_call(
        functools.partial(combine_kernel, repeat=repeat, heads=kv_heads * repeat),
        out_shape=jax.ShapeDtypeStruct((copies, rows, width), BF16),
        grid=(kv_heads,),
        in_specs=[
            pl.BlockSpec(memory_space=pltpu.SMEM),
            pl.BlockSpec((sources, rows, part), lambda k: (0, 0, k)),
            pl.BlockSpec((sources, rows, LANES), lambda k: (0, 0, width // LANES)),
            pl.BlockSpec((rows, part), lambda k: (0, k)),
            pl.BlockSpec((TREE_NODES, HEAD_SIZE), lambda k: (0, k)),
            pl.BlockSpec((TREE_NODES, HEAD_SIZE), lambda k: (0, k)),
            pl.BlockSpec((TREE_NODES, TREE_NODES), lambda k: (0, 0)),
        ],
        out_specs=pl.BlockSpec((copies, rows, part), lambda k: (0, 0, k)),
        compiler_params=vmem(VMEM_MIB),
        cost_estimate=pl.CostEstimate(
            flops=4 * rows * width * TREE_NODES,
            bytes_accessed=2 * recv.size + 4 * rows * width,
            transcendentals=rows * width // 2,
        ),
        name=name,
    )(path_nodes, recv, recv, queries, tree_keys, tree_values, mask)


def fold_kernel(*refs, repeat):
    sources, o_ref = refs[:-1], refs[-1]
    rows = o_ref.shape[1]
    part = repeat * HEAD_SIZE
    lane = lax.broadcasted_iota(jnp.int32, (rows, LANES), 1)
    stats = [join_lanes(ref[0, :, part:], repeat) for ref in sources]
    best = functools.reduce(jnp.maximum, stats)
    scales = [jnp.exp2(stat - best) for stat in stats]
    total = functools.reduce(jnp.add, scales)
    for i in range(repeat):
        cols = slice(i * HEAD_SIZE, (i + 1) * HEAD_SIZE)

        def column(stat):
            return jnp.sum(jnp.where(lane == i, stat, 0.0), axis=1, keepdims=True)

        numer = 0.0
        for ref, scale in zip(sources, scales):
            numer += column(scale) * ref[0, :, cols].astype(F32)
        o_ref[0, :, cols] = (numer / column(total)).astype(BF16)
    lse = best + jnp.log(total) * LOG2E
    o_ref[0, :, part:] = split_lanes(jnp.where(lane < repeat, lse, 0.0), repeat)


def fold_blocks(sources, first, count, repeat):
    _, rows, wide = sources[0].shape
    return pl.pallas_call(
        functools.partial(fold_kernel, repeat=repeat),
        out_shape=jax.ShapeDtypeStruct((count, rows, wide), BF16),
        grid=(count,),
        in_specs=[
            pl.BlockSpec((1, rows, wide), lambda j: (first + 2 * j, 0, 0)) for _ in sources
        ],
        out_specs=pl.BlockSpec((1, rows, wide), lambda j: (j, 0, 0)),
        compiler_params=vmem(VMEM_MIB),
        cost_estimate=pl.CostEstimate(
            flops=rows * wide, bytes_accessed=6 * rows * wide, transcendentals=0
        ),
        name="fold_blocks",
    )(*sources)


def pair_kernel(place_ref, *refs, repeat):
    count = (len(refs) - 5) // 2
    near, far, rest = refs[:count], refs[count:-5], refs[-5:]
    q_ref, k_ref, v_ref, mask_ref, o_ref = rest
    part = repeat * HEAD_SIZE
    for turn in range(2):

        @pl.when(pl.program_id(0) == turn)
        def _(turn=turn):
            mine = [ref.at[0] for ref in (near if turn == 0 else far)]
            merge_heads(
                [
                    lambda i, ref=ref: ref[:, i * HEAD_SIZE : (i + 1) * HEAD_SIZE]
                    for ref in mine
                ],
                [join_lanes(ref[:, part:], repeat) for ref in mine],
                0,
                q_ref,
                k_ref,
                v_ref,
                mask_ref[...],
                o_ref,
                repeat,
            )


def combine_pair(place, near, far, queries, tree_keys, tree_values, mask, repeat):
    rows, width = queries.shape
    part = repeat * HEAD_SIZE
    wide = far[0].shape[2]

    def head(j, p):
        return (0, p[0] % 2 ^ j)

    return pl.pallas_call(
        functools.partial(pair_kernel, repeat=repeat),
        out_shape=jax.ShapeDtypeStruct((1, rows, width), BF16),
        grid_spec=pltpu.PrefetchScalarGridSpec(
            num_scalar_prefetch=1,
            grid=(2,),
            in_specs=[pl.BlockSpec((1, rows, wide), lambda j, p: (0, 0, 0)) for _ in near + far]
            + [
                pl.BlockSpec((rows, part), head),
                pl.BlockSpec((TREE_NODES, HEAD_SIZE), head),
                pl.BlockSpec((TREE_NODES, HEAD_SIZE), head),
                pl.BlockSpec((rows, TREE_NODES), lambda j, p: (0, 0)),
            ],
            out_specs=pl.BlockSpec((1, rows, part), lambda j, p: (0, 0, p[0] % 2 ^ j)),
        ),
        compiler_params=vmem(VMEM_MIB),
        cost_estimate=pl.CostEstimate(
            flops=4 * rows * width * TREE_NODES,
            bytes_accessed=8 * rows * width,
            transcendentals=rows * width // 2,
        ),
        name="combine_pair",
    )(place, *near, *far, queries, tree_keys, tree_values, mask)


def fc_kernel(length_ref, feat_ref, wn_hbm, wp_hbm, o_ref, wn_ref, wp_ref, sems):
    count, block, _ = wn_ref.shape
    copies = []
    for i in range(count):
        rows = pl.ds(i * block, block)
        copies.append(
            (
                pltpu.make_async_copy(wn_hbm.at[rows], wn_ref.at[i], sems.at[0, i]),
                pltpu.make_async_copy(wp_hbm.at[rows], wp_ref.at[i], sems.at[1, i]),
            )
        )
        for copy in copies[-1]:
            copy.start()
    feats = feat_ref[...]
    live, slots = o_ref.shape[0], feats.shape[0]
    shape = (live, slots)
    place, child, step = live_places(length_ref, slots // ACCEPT, shape, 1)
    row = lax.broadcasted_iota(jnp.int32, shape, 0)
    pick = place == row
    prev = (child == row) | ((step == 0) & pick)
    node = dot_nn(pick.astype(F32).astype(BF16), feats).astype(BF16)
    parent = dot_nn(prev.astype(F32).astype(BF16), feats).astype(BF16)
    total = jnp.zeros(o_ref.shape, F32)
    for i in range(count):
        cols = slice(i * block, (i + 1) * block)
        for copy in copies[i]:
            copy.wait()
        total += dot_nn(node[:, cols], wn_ref[i]) + dot_nn(parent[:, cols], wp_ref[i])
    o_ref[...] = total


def fc_project(feats, path_lengths, fc_node, fc_parent):
    slots, width = feats.shape
    live = slots // 2
    cols = fc_node.shape[1]
    block = min(width, 512)
    count = width // block
    return pl.pallas_call(
        fc_kernel,
        out_shape=jax.ShapeDtypeStruct((live, cols), F32),
        in_specs=[
            pl.BlockSpec(memory_space=pltpu.SMEM),
            pl.BlockSpec(memory_space=pltpu.VMEM),
            pl.BlockSpec(memory_space=pl.ANY),
            pl.BlockSpec(memory_space=pl.ANY),
        ],
        scratch_shapes=[
            pltpu.VMEM((count, block, cols), BF16),
            pltpu.VMEM((count, block, cols), BF16),
            pltpu.SemaphoreType.DMA((2, count)),
        ],
        compiler_params=vmem(VMEM_MIB),
        cost_estimate=pl.CostEstimate(
            flops=4 * live * width * cols, bytes_accessed=4 * width * cols, transcendentals=0
        ),
        name="fc_project",
    )(path_lengths, feats, fc_node, fc_parent)


def gate_kernel(xa_ref, xb_ref, gain_ref, wg_ref, wu_ref, o_ref):
    x = xa_ref[...] + xb_ref[...]
    together = o_ref.shape[0]
    units = wg_ref.shape[1] // together
    scaled = (x * gain_ref[...]).astype(BF16)
    squares = jnp.sum(x * x, axis=1, keepdims=True)
    lane = lax.broadcasted_iota(jnp.int32, (x.shape[0], LANES), 1)
    tail = split_lanes(jnp.where(lane == 0, squares, 0.0), 1)
    for t in range(together):
        cols = slice(t * units, (t + 1) * units)
        o_ref[t, :, :units] = dot_nn(scaled, wg_ref[:, cols]).astype(BF16)
        o_ref[t, :, units : 2 * units] = dot_nn(scaled, wu_ref[:, cols]).astype(BF16)
        o_ref[t, :, 2 * units :] = tail


def gate_up(xa, xb, gain, w_gate, w_up, parts):
    live, width = xa.shape
    units = w_gate.shape[1] // parts
    together = 2 if parts % 2 == 0 else 1
    return pl.pallas_call(
        gate_kernel,
        out_shape=jax.ShapeDtypeStruct((parts, live, 2 * units + LANES), BF16),
        grid=(parts // together,),
        in_specs=[
            pl.BlockSpec((live, width), lambda i: (0, 0)),
            pl.BlockSpec((live, width), lambda i: (0, 0)),
            pl.BlockSpec((1, width), lambda i: (0, 0)),
            pl.BlockSpec((width, together * units), lambda i: (0, i)),
            pl.BlockSpec((width, together * units), lambda i: (0, i)),
        ],
        out_specs=pl.BlockSpec((together, live, 2 * units + LANES), lambda i: (i, 0, 0)),
        compiler_params=vmem(VMEM_MIB),
        cost_estimate=pl.CostEstimate(
            flops=4 * live * width * units * parts,
            bytes_accessed=4 * width * units * parts,
            transcendentals=0,
        ),
        name="gate_up",
    )(xa, xb, gain, w_gate, w_up)


def act_kernel(recv_ref, o_ref):
    units = o_ref.shape[2]
    sources = recv_ref.shape[0]
    total = recv_ref[0].astype(F32)
    for c in range(1, sources):
        total += recv_ref[c].astype(F32)
    squares = jnp.sum(total[:, 2 * units :], axis=1, keepdims=True)
    scale = lax.rsqrt(squares / MODEL_WIDTH + 1e-05)
    gate = total[:, :units] * scale
    up = total[:, units : 2 * units] * scale
    hidden = (gate / (1.0 + jnp.exp(-gate)) * up).astype(BF16)
    for c in range(sources):
        o_ref[c] = hidden


def activate(recv):
    sources, live, wide = recv.shape
    units = (wide - LANES) // 2
    return pl.pallas_call(
        act_kernel,
        out_shape=jax.ShapeDtypeStruct((sources, live, units), BF16),
        compiler_params=vmem(VMEM_MIB),
        cost_estimate=pl.CostEstimate(
            flops=recv.size, bytes_accessed=3 * recv.size, transcendentals=live * units
        ),
        name="activate",
    )(recv)


def down_kernel(head_ref, length_ref, hid_ref, xa_ref, xb_ref, w_hbm, *refs):
    outs, w_ref, sems = refs[:-2], refs[-2], refs[-1]
    parts, units, _ = w_ref.shape
    copies = [
        pltpu.make_async_copy(w_hbm.at[pl.ds(i * units, units)], w_ref.at[i], sems.at[i])
        for i in range(parts)
    ]
    for copy in copies:
        copy.start()
    total = jnp.where(head_ref[0] == 0, xa_ref[...] + xb_ref[...], 0.0)
    live = total.shape[0]
    share = outs[0].shape[0]
    for i in range(parts):
        copies[i].wait()
        total += dot_nn(hid_ref[i], w_ref[i])
    for k, out in enumerate(outs):
        place, _, _ = live_places(
            length_ref, 2 * live // ACCEPT, (share, live), 0, (head_ref[0] ^ k) * share
        )
        spread = (place == lax.broadcasted_iota(jnp.int32, (share, live), 1)).astype(F32)
        out[...] = lax.dot_general(
            spread,
            total,
            (((1,), (0,)), ((), ())),
            precision=lax.Precision.HIGHEST,
            preferred_element_type=F32,
        )


def down_project(head, path_lengths, hidden, w_down, xa, xb, shares):
    parts, live, units = hidden.shape
    cols = w_down.shape[1]
    return pl.pallas_call(
        down_kernel,
        out_shape=[jax.ShapeDtypeStruct((2 * live // shares, cols), F32)] * shares,
        in_specs=[pl.BlockSpec(memory_space=pltpu.SMEM)] * 2
        + [pl.BlockSpec(memory_space=pltpu.VMEM)] * 3
        + [pl.BlockSpec(memory_space=pl.ANY)],
        scratch_shapes=[
            pltpu.VMEM((parts, units, cols), BF16),
            pltpu.SemaphoreType.DMA((parts,)),
        ],
        compiler_params=vmem(VMEM_MIB),
        cost_estimate=pl.CostEstimate(
            flops=2 * live * parts * units * cols,
            bytes_accessed=2 * parts * units * cols,
            transcendentals=0,
        ),
        name="down_project",
    )(head, path_lengths, hidden, xa, xb, w_down)


def swap(blocks, axis):
    return lax.all_to_all(blocks, axis, split_axis=0, concat_axis=0, tiled=True)


def spread_all(block, axis):
    count = lax.axis_size(axis)
    return swap(jnp.broadcast_to(block[None], (count,) + block.shape), axis)


def partner(value, axis, distance):
    count = lax.axis_size(axis)
    return lax.ppermute(value, axis, [(i, i ^ distance) for i in range(count)])


def shards(
    queries,
    draft_node_keys,
    draft_node_values,
    prompt_keys,
    prompt_values,
    request_group,
    parents,
    node_visibility_mask,
    path_nodes,
    path_lengths,
    fc_node,
    fc_parent,
    norm_gain,
    w_gate,
    w_up,
    w_down,
):
    ctx_count = lax.axis_size("ctx")
    head_count = lax.axis_size("head")
    requests = request_group.shape[0]
    kv_heads = draft_node_keys.shape[1] // HEAD_SIZE
    width = queries.shape[1]
    repeat = width // HEAD_SIZE // kv_heads
    slots = requests * ACCEPT

    paired = kv_heads == 2 and ctx_count % 2 == 0
    me = lax.axis_index("ctx")
    place = me.reshape(1)
    paired = paired and requests == ctx_count == 8
    if paired:
        part = repeat * HEAD_SIZE
        halves = jnp.stack([queries[:, :part], queries[:, part:]])
        outgoing = jnp.broadcast_to(
            halves[None], (ctx_count // 2,) + halves.shape
        ).reshape(ctx_count, TREE_NODES, part)
    else:
        outgoing = None

    mask = node_visibility_mask[0]
    path_spread, path_queries = path_rows(path_nodes, queries, ctx_count)
    path_all = swap(path_spread, "ctx").reshape(slots, width)
    path_part, *traded = path_attend(
        path_all, prompt_keys, prompt_values, request_group, place, kv_heads, repeat, int(paired)
    )
    path_recv = swap(path_part.reshape(requests, ACCEPT, width + LANES), "ctx")
    if paired:
        far_keys, far_values = (partner(block, "ctx", 1) for block in traded)
    features = combine(
        path_nodes,
        path_recv,
        path_queries,
        draft_node_keys,
        draft_node_values,
        mask,
        kv_heads,
        repeat,
        ctx_count,
        "path_combine",
    )
    every_row = swap(features, "ctx").reshape(slots, width)
    if paired:
        every_row, outgoing, far_keys = lax.optimization_barrier((every_row, outgoing, far_keys))
        blocks = [prompt_keys, prompt_values, far_keys, far_values]
        bulk_queries = swap(outgoing, "ctx")
    else:
        blocks = [prompt_keys, prompt_values]
        bulk_queries = lax.all_gather(queries, "ctx", axis=0)

    x_total = fc_project(every_row, path_lengths, fc_node, fc_parent)
    distance = 1
    x_other = jnp.zeros_like(x_total)
    while distance < head_count:
        if distance > 1:
            x_total = x_total + x_other
        x_other = partner(x_total, "head", distance)
        distance *= 2

    units = w_gate.shape[1] // ctx_count
    gain = norm_gain[None, :]
    by_lanes = units % LANES == 0
    if by_lanes:
        partial = gate_up(x_total, x_other, gain, w_gate, w_up, ctx_count)
        if paired:
            partial, bulk_queries, *blocks[2:] = lax.optimization_barrier(
                (partial, bulk_queries, *blocks[2:])
            )
        summed = swap(partial, "ctx")
    else:
        x = x_total + x_other
        scaled = (x * gain).astype(BF16)
        both = jnp.stack(
            [
                jnp.dot(scaled, w_gate, preferred_element_type=F32),
                jnp.dot(scaled, w_up, preferred_element_type=F32),
            ]
        )
        both = lax.psum_scatter(both, "ctx", scatter_dimension=2, tiled=True)
        squares = lax.psum(jnp.sum(x * x, axis=1), "ctx")
        summed = both * lax.rsqrt(squares / MODEL_WIDTH + 1e-05)[None, :, None]

    if paired:
        sent = bulk_attend(bulk_queries, blocks, request_group, place, repeat, 1)
        sent, place = lax.optimization_barrier((sent, place))
        kept = bulk_attend(bulk_queries, blocks, request_group, place, repeat, 0)
        near = partner(sent, "ctx", 2)
        summed, kept = lax.optimization_barrier((summed, kept))
    else:
        parts = []
        for k in range(kv_heads):
            cols = slice(k * HEAD_SIZE, (k + 1) * HEAD_SIZE)
            heads = slice(k * repeat * HEAD_SIZE, (k + 1) * repeat * HEAD_SIZE)
            part = bulk_attend(
                bulk_queries[:, :, heads],
                [block[:, :, cols] for block in blocks],
                request_group,
                place,
                repeat,
                None,
            )
            parts.append(
                combine(
                    path_nodes,
                    swap(part, "ctx"),
                    queries[:, heads],
                    draft_node_keys[:, cols],
                    draft_node_values[:, cols],
                    mask,
                    1,
                    repeat,
                    1,
                    "bulk_combine",
                )[0]
            )
        attention_fn = jnp.concatenate(parts, axis=1)

    if by_lanes:
        hidden = activate(summed)
        if paired:
            hidden, near = lax.optimization_barrier((hidden, near))
        hidden_all = swap(hidden, "ctx")
        if paired:
            halves = [kept, near]
            across = [partner(fold_blocks(halves, n, 1, repeat), "ctx", 1) for n in (3, 1)]
            further = fold_blocks(halves, 2, 1, repeat)
            mine = fold_blocks(halves, 0, 1, repeat)
            hidden_all, across[0], further, mine = lax.optimization_barrier(
                (hidden_all, across[0], further, mine)
            )
            last = [partner(block, "ctx", 4) for block in (further, across[0])]
    else:
        hidden = (jax.nn.silu(summed[0]) * summed[1]).astype(BF16)
        hidden_all = lax.all_gather(hidden, "ctx", axis=1, tiled=True)[None]
    head = lax.axis_index("head").reshape(1)
    expanded = down_project(head, path_lengths, hidden_all, w_down, x_total, x_other, head_count)
    if paired:
        expanded, across[1], last = lax.optimization_barrier((expanded, across[1], last))
        attention_fn = combine_pair(
            place, [mine, last[0]], [across[1], last[1]], queries, draft_node_keys, draft_node_values, mask, repeat
        )[0]
    pieces = [expanded[0]] + [partner(expanded[k], "head", k) for k in range(1, head_count)]
    draft_out = functools.reduce(jnp.add, pieces).astype(BF16)
    return (attention_fn, draft_out)


def solution(mesh):
    return jax.shard_map(
        shards,
        mesh=mesh,
        in_specs=(
            P("ctx", "head"),
            P("ctx", "head"),
            P("ctx", "head"),
            P(None, "ctx", "head"),
            P(None, "ctx", "head"),
            P(),
            P("ctx", None),
            P("ctx", None, None),
            P("ctx", None),
            P(),
            P("head", "ctx"),
            P("head", "ctx"),
            P("ctx"),
            P("ctx", "head"),
            P("ctx", "head"),
            P("head", "ctx"),
        ),
        out_specs=(P("ctx", "head"), P("head", "ctx")),
        check_vma=False,
    )
```
